32 devices in a mesh: seq: 8 (over z, y), head: 4 (over x, core).
Axes of the slice: x: 2, y: 2, z: 4, core: 2. Of those that a mesh axis runs over, the one named last changes fastest.
Arguments:
- queries: bfloat16 [4096, 32, 128], P('seq', 'head'), may hold values from -6 to 6
- key_vectors: bfloat16 [4096, 32, 128], P('seq', 'head'), may hold values from -6 to 6
- value_vectors: bfloat16 [4096, 32, 128], P('seq', 'head'), may hold values from -6 to 6
- doc_ids: int32 [4096], P('seq'), may hold values from 0 to 2, never falling along the last dimension, each value on 1 to 2048 neighbouring positions
- out_weight: bfloat16 [4096, 3072], P('head'), may hold values from -0.09375 to 0.09375
- grad_out: bfloat16 [4096, 3072], P('seq', 'head'), may hold values from -6 to 6
Outputs:
- layer_out: bfloat16 [4096, 3072], P('seq', 'head')
- grad_queries: bfloat16 [4096, 32, 128], P('seq', 'head')
- grad_keys: bfloat16 [4096, 32, 128], P('seq', 'head')
- grad_values: bfloat16 [4096, 32, 128], P('seq', 'head')
- grad_weight: float32 [4096, 3072], P('head', 'seq')
The draws below stay inside these ranges and needn't reach their ends.
Inputs may be any that keep to these rules, and one draw needn't show every extreme that they name: doc_ids never falls; each of the 3 documents has 1 to 2048 tokens and one has exactly 2048.
All inputs are finite; a program needn't handle non-finite values.
Results may differ from the reference program's by a relative error of at most 0.0063.
Values may be sent and summed in bfloat16 or wider, within the bound.
A program may use at most 128 MiB of HBM per device.

```python
import math
import jax
import jax.numpy as jnp
import numpy as np
from jax import lax

DH = 128
HEADS = 32
DM = 3072
TOK_DEV = 512
TOKENS = 4096
HD = 4096
DOCS = 3
DOC_MOST = 2048


def steps_of(key, shape, shards, smallest, high):
    def one(position, blocks):
        heights = jax.random.uniform(jax.random.fold_in(jax.random.fold_in(key, 6), position), (blocks,), jnp.float32, smallest / len(shards), high / len(shards))
        return jnp.repeat(jnp.exp(heights), shape[position] // blocks).reshape((-1,) + (1,) * (len(shape) - position - 1))

    level = one(*shards[0])
    for cut in shards[1:]:
        level = level * one(*cut)
    return level


def length_profile(count, total, bound, slope):
    loads = [(1 << 20) // math.isqrt(grade ** slope) + 1 for grade in range(2, count + 1)]
    rest, counts = total - bound - (count - 1), [1] * (count - 1)
    while rest > 0:
        candidates = [i for i in range(count - 1) if counts[i] < bound]
        pool, left = sum([loads[i] for i in candidates]), rest
        for i in candidates:
            addition = min(bound - counts[i], max(1, left * loads[i] // pool), rest)
            counts[i] = counts[i] + addition
            rest = rest - addition
    return np.array([bound] + counts)


def ragged(stream_key, count, total, bound, lean):
    if count == 2:
        one = jax.random.randint(stream_key, (), max(1, total - bound), min(bound, total - 1) + 1)
        return jnp.stack([one, total - one])
    lengths = jnp.asarray(length_profile(count, total, bound, lean), jnp.int32)
    couples = (count - 1) // 2
    source_of, taker = lengths[1:1 + 2 * couples:2], lengths[2:2 + 2 * couples:2]
    margin = jnp.minimum(source_of - 1, bound - taker)
    shifted = jax.random.randint(jax.random.fold_in(stream_key, 1), (couples,), 0, 1 << 20) % (margin + 1)
    lengths = lengths.at[1:1 + 2 * couples:2].set(source_of - shifted).at[2:2 + 2 * couples:2].set(taker + shifted)
    return lengths[jax.random.permutation(jax.random.fold_in(stream_key, 2), count)]


def scatter_about(own_key, extent, scale, most, shards=(), held_as=jnp.bfloat16):
    entries = scale * jax.random.normal(own_key, extent, jnp.float32)
    if shards:
        entries = entries * steps_of(own_key, extent, shards, -0.22, 0.18)
    return jnp.clip(entries, -most, most).astype(held_as)


def setup_inputs(seed: int = 0) -> dict:
    seeds = jax.random.split(jax.random.key(seed), 7)
    queries = scatter_about(seeds[0], (TOKENS, HEADS, DH), 1.0, 6.0, ((0, 8), (1, 4)))
    key_vectors = scatter_about(seeds[1], (TOKENS, HEADS, DH), 1.0, 6.0, ((0, 8), (1, 4)))
    value_vectors = scatter_about(seeds[2], (TOKENS, HEADS, DH), 1.0, 6.0, ((0, 8), (1, 4)))
    doc_ids = jnp.searchsorted(jnp.cumsum(ragged(seeds[3], DOCS, TOKENS, DOC_MOST, 0)), jnp.arange(TOKENS), side="right").astype(jnp.int32)
    out_weight = scatter_about(seeds[4], (HD, DM), HD ** -0.5, 0.09375, ((0, 4),))
    grad_out = scatter_about(seeds[5], (TOKENS, DM), 1.0, 6.0, ((0, 8), (1, 4)))
    return {"queries": queries, "key_vectors": key_vectors, "value_vectors": value_vectors, "doc_ids": doc_ids, "out_weight": out_weight, "grad_out": grad_out}


def combine(earlier, later):
    same = (earlier[0] == later[0]).astype(jnp.float32)
    return (later[0], later[1] + same[0] * earlier[1])

def reference(queries, key_vectors, value_vectors, doc_ids, out_weight, grad_out):
    blocks = TOKENS // TOK_DEV
    query_blocks = queries.reshape(blocks, TOK_DEV, HEADS, DH)
    key_blocks = key_vectors.reshape(blocks, TOK_DEV, HEADS, DH)
    value_blocks = value_vectors.reshape(blocks, TOK_DEV, HEADS, DH)
    doc_blocks = doc_ids.astype(jnp.float32).reshape(blocks, TOK_DEV)
    causal = lax.broadcasted_iota(jnp.int32, (TOK_DEV, TOK_DEV), 0) >= lax.broadcasted_iota(jnp.int32, (TOK_DEV, TOK_DEV), 1)
    start = (jnp.full((1,), -1.0, jnp.float32), jnp.zeros((HEADS, DH, DH), jnp.float32))

    def scores_of(query_f, key_f, doc_row):
        pairs = causal & (doc_row[:, None] == doc_row[None, :])
        scores = jnp.einsum('thd,shd->hts', query_f, key_f)
        return (jnp.where(pairs[None], scores, 0.0).astype(jnp.bfloat16), pairs)

    def forward_step(carry, inputs):
        query_blk, key_blk, value_blk, doc_row = inputs
        query_f = query_blk.astype(jnp.float32)
        key_f = key_blk.astype(jnp.float32)
        value_f = value_blk.astype(jnp.float32)
        state_low = carry[1].astype(jnp.bfloat16).astype(jnp.float32)
        reads = (doc_row == carry[0][0]).astype(jnp.float32)
        scores_low, pairs = scores_of(query_f, key_f, doc_row)
        attn = jnp.einsum('hts,she->the', scores_low.astype(jnp.float32), value_f)
        attn = attn + reads[:, None, None] * jnp.einsum('thd,hde->the', query_f, state_low)
        tail = (doc_row == doc_row[-1]).astype(jnp.float32)
        own_state = jnp.einsum('shd,she->hde', key_f * tail[:, None, None], value_f)
        return (combine(carry, (doc_row[-1:], own_state)), (attn, carry[1], carry[0]))
    last_carry, (attn, state_in, prev_doc) = lax.scan(forward_step, start, (query_blocks, key_blocks, value_blocks, doc_blocks))
    attn = attn.reshape(TOKENS, HEADS, DH)
    scale = lax.rsqrt(lax.optimization_barrier(jnp.mean(attn * attn, axis=-1, keepdims=True)) + 1e-05)
    normed_f = attn * scale
    normed = normed_f.astype(jnp.bfloat16).reshape(TOKENS, HD)
    layer_out = jnp.dot(normed, out_weight, preferred_element_type=jnp.float32).astype(jnp.bfloat16)
    grad_normed = lax.dot_general(grad_out, out_weight, (((1,), (1,)), ((), ())), preferred_element_type=jnp.float32).reshape(TOKENS, HEADS, DH)
    grad_attn = (scale * (grad_normed - normed_f * lax.optimization_barrier(jnp.mean(grad_normed * normed_f, axis=-1, keepdims=True)))).astype(jnp.bfloat16)
    grad_weight = lax.dot_general(normed, grad_out, (((0,), (0,)), ((), ())), preferred_element_type=jnp.float32)
    grad_blocks = grad_attn.reshape(blocks, TOK_DEV, HEADS, DH)

    def backward_step(carry, inputs):
        query_blk, key_blk, value_blk, doc_row, grad_blk, state_blk, prev_blk = inputs
        query_f = query_blk.astype(jnp.float32)
        key_f = key_blk.astype(jnp.float32)
        value_f = value_blk.astype(jnp.float32)
        grad_f = grad_blk.astype(jnp.float32)
        state_low = state_blk.astype(jnp.bfloat16).astype(jnp.float32)
        back_low = carry[1].astype(jnp.bfloat16).astype(jnp.float32)
        reads = (doc_row == prev_blk[0]).astype(jnp.float32)
        writes = (doc_row == carry[0][0]).astype(jnp.float32)
        scores_low, pairs = scores_of(query_f, key_f, doc_row)
        grad_scores = jnp.einsum('the,she->hts', grad_f, value_f)
        grad_scores = jnp.where(pairs[None], grad_scores, 0.0).astype(jnp.bfloat16).astype(jnp.float32)
        grad_q = jnp.einsum('hts,shd->thd', grad_scores, key_f) + reads[:, None, None] * jnp.einsum('the,hde->thd', grad_f, state_low)
        grad_k = jnp.einsum('hts,thd->shd', grad_scores, query_f) + writes[:, None, None] * jnp.einsum('she,hde->shd', value_f, back_low)
        grad_v = jnp.einsum('hts,the->she', scores_low.astype(jnp.float32), grad_f) + writes[:, None, None] * jnp.einsum('shd,hde->she', key_f, back_low)
        head_mask = (doc_row == doc_row[0]).astype(jnp.float32)
        own_state = jnp.einsum('thd,the->hde', query_f * head_mask[:, None, None], grad_f)
        outs = (grad_q.astype(jnp.bfloat16), grad_k.astype(jnp.bfloat16), grad_v.astype(jnp.bfloat16))
        return (combine(carry, (doc_row[:1], own_state)), outs)
    final_carry, (grad_q, grad_k, grad_v) = lax.scan(backward_step, start, (query_blocks, key_blocks, value_blocks, doc_blocks, grad_blocks, state_in, prev_doc), reverse=True)
    shape = (TOKENS, HEADS, DH)
    return (layer_out, grad_q.reshape(shape), grad_k.reshape(shape), grad_v.reshape(shape), grad_weight)
```

```python
import functools

import jax
import jax.numpy as jnp
from jax import lax
from jax.experimental import pallas as pl
from jax.experimental.pallas import tpu as pltpu
from jax.sharding import PartitionSpec as P


BF = jnp.bfloat16
F32 = jnp.float32
MESH = pl.DeviceIdType.MESH


def dot_nn(a, b):
    return lax.dot_general(a, b, (((1,), (0,)), ((), ())), preferred_element_type=F32)


def dot_nt(a, b):
    return lax.dot_general(a, b, (((1,), (1,)), ((), ())), preferred_element_type=F32)


def dot_tn(a, b):
    return lax.dot_general(a, b, (((0,), (0,)), ((), ())), preferred_element_type=F32)


def loop(count, body):
    lax.fori_loop(0, count, lambda i, _: (body(i), None)[1], None)


def kernel(
    sizes,
    docs_ref, q_hbm, k_hbm, v_hbm, w_hbm, go_hbm,
    lo_out, gq_out, gk_out, gv_out, gw_out,
    q, k, v, w, g, p, mask, scores, attn, gn, normed, nt, ntp, ga,
    f_own, f_near, f_far, f_sum, f_last, f_low,
    r_own, r_near, r_far, r_sum, r_last, r_low,
    lc_send, lc_recv, lx_send, lx_recv, lo_acc, lo_fin,
    sb, ub, db, gacc, part, gq, gk, gv,
    doc_col, reads, writes, tail, front,
    in_sem, g_send, g_recv, p_send, p_recv, f_send, f_recv, r_send, r_recv,
    n_send, n_recv, lc_ss, lc_rs, lx_ss, lx_rs, u_ss, u_rs, d_ss, d_rs, out_sem,
):
    n, m, heads, length, dh, share, width = sizes
    line = n // 2
    pairs = heads // 2
    rows = 2 * dh
    tile = 2 * dh
    s = lax.axis_index("seq")
    h = lax.axis_index("head")
    a = s // 2
    b = s % 2
    hc = h % 2
    hx = h // 2
    core = h + 1 - 2 * hc
    across = h + 2 - 4 * hx
    both = core + 2 - 4 * hx
    mate = s + 1 - 2 * b

    barrier = pltpu.get_barrier_semaphore()

    def greet(seq, head):
        pl.semaphore_signal(barrier, inc=1, device_id=(seq, head), device_id_type=MESH)

    def local(src, dst, i):
        return pltpu.make_async_copy(src, dst, in_sem.at[i])

    def remote(src, dst, ss, rs, seq, head):
        return pltpu.make_async_remote_copy(
            src_ref=src, dst_ref=dst, send_sem=ss, recv_sem=rs,
            device_id=(seq, head), device_id_type=MESH,
        )

    loads = [
        local(go_hbm, g.at[h], 0), local(k_hbm, k, 1), local(v_hbm, v, 2),
        local(q_hbm, q, 3), local(w_hbm, w, 4),
    ]
    for copy in loads:
        copy.start()
    greet(s, core)
    greet(s, across)
    for step in (1, 2):
        @pl.when(s + step < n)
        def _():
            greet(s + step, h)

        @pl.when(s >= step)
        def _():
            greet(s - step, h)

    def spot(cond):
        return jnp.where(cond, 1, 0)

    docs_row = docs_ref[...].astype(F32)
    doc_col[...] = jnp.broadcast_to(docs_row, (dh, length)).T
    for i in range(length // dh):
        at = pl.ds(i * dh, dh)
        col = doc_col[at, :][:, :1]
        t_pos = lax.broadcasted_iota(jnp.int32, (dh, length), 0) + i * dh
        s_pos = lax.broadcasted_iota(jnp.int32, (dh, length), 1)
        ok = (t_pos >= s_pos) & (col == docs_row)
        mask[at, :] = jnp.where(ok, 1.0, 0.0).astype(BF)
    last_doc = doc_col[pl.ds(length - 1, 1), :]
    first_doc = doc_col[pl.ds(0, 1), :]
    tail[...] = jnp.where(doc_col[...] == last_doc, 1.0, 0.0).astype(BF)
    front[...] = jnp.where(doc_col[...] == first_doc, 1.0, 0.0).astype(BF)
    for c in range(pairs):
        f_own[c, pl.ds(rows, 16), :] = jnp.broadcast_to(last_doc, (16, dh)).astype(BF)
        r_own[c, pl.ds(rows, 16), :] = jnp.broadcast_to(first_doc, (16, dh)).astype(BF)

    def blank(near, far, last, place):
        for ref, least in ((near, 1), (far, 2), (last, 3)):
            @pl.when(place < least)
            def _():
                ref[...] = jnp.zeros_like(ref)
                for c in range(pairs):
                    ref[c, pl.ds(rows, 16), :] = jnp.full((16, dh), -1.0, BF)

    blank(f_near, f_far, f_last, s)
    blank(r_near, r_far, r_last, n - 1 - s)

    pl.semaphore_wait(
        barrier, 2 + spot(s + 1 < n) + spot(s + 2 < n) + spot(s >= 1) + spot(s >= 2)
    )

    loads[0].wait()
    g_core = remote(g.at[h], g.at[h], g_send.at[0], g_recv.at[0], s, core)
    g_across = remote(g.at[h], g.at[h], g_send.at[1], g_recv.at[1], s, across)
    g_pass = remote(g.at[across], g.at[across], g_send.at[2], g_recv.at[2], s, core)
    p_mate = remote(
        g.at[h, :, pl.ds(pl.multiple_of((1 - b) * width, 128), width)], p.at[h],
        p_send.at[0], p_recv.at[0], mate, h,
    )
    p_core = remote(p.at[h], p.at[h], p_send.at[1], p_recv.at[1], s, core)
    p_across = remote(p.at[h], p.at[h], p_send.at[2], p_recv.at[2], s, across)
    p_pass = remote(p.at[across], p.at[across], p_send.at[3], p_recv.at[3], s, core)
    g_across.start()
    p_mate.start()
    g_core.start()

    class States:
        def __init__(self, sign, place, own, near, far, total, last, ss, rs):
            self.refs = own, near, far, total, last
            self.sign, self.place, self.ss, self.rs = sign, place, ss, rs

        def copy(self, kind, c):
            own, near, far, total, last = self.refs
            src = total if kind == 2 else own
            dst = (near, far, last)[kind]
            step = 1 if kind == 0 else 2
            return remote(
                src.at[c], dst.at[c], self.ss.at[kind, c], self.rs.at[kind, c],
                s + self.sign * step, h,
            )

        def sends(self, kind):
            if kind == 0:
                return self.place + 1 < n
            if kind == 1:
                return self.place + 2 < n
            return (self.place + 2 < n) & (self.place >= 1)

        def gets(self, kind):
            return self.place >= kind + 1

        def send(self, kind, c):
            @pl.when(self.sends(kind))
            def _():
                self.copy(kind, c).start()

        def wait(self, kind, c):
            @pl.when(self.gets(kind))
            def _():
                self.copy(kind, c).wait_recv()

        def sent(self, kind, c):
            @pl.when(self.sends(kind))
            def _():
                self.copy(kind, c).wait_send()

        def join(self, base, more, c):
            same = base[c, pl.ds(rows, 1), :] == more[c, pl.ds(rows, 1), :]
            held = base[c, pl.ds(0, rows), :].astype(F32)
            extra = more[c, pl.ds(0, rows), :].astype(F32)
            same = jnp.broadcast_to(same.astype(F32), (rows, dh))
            return held + extra * same

        def first(self, c):
            own, near, far, total, last = self.refs
            self.wait(0, c)
            self.wait(1, c)
            total[c, pl.ds(0, rows), :] = self.join(near, far, c).astype(BF)
            total[c, pl.ds(rows, 16), :] = near[c, pl.ds(rows, 16), :]
            self.send(2, c)

        def second(self, c, low):
            own, near, far, total, last = self.refs
            self.wait(2, c)
            both = self.join(total, last, c).astype(BF)
            low[2 * c] = both[:dh]
            low[2 * c + 1] = both[dh:]

        def reached(self):
            total = self.refs[3]
            doc = total[0, pl.ds(rows, 1), :].astype(F32)
            return jnp.where(doc_col[...] == doc, 1.0, 0.0)

    ahead = States(1, s, f_own, f_near, f_far, f_sum, f_last, f_send, f_recv)
    behind = States(-1, n - 1 - s, r_own, r_near, r_far, r_sum, r_last, r_send, r_recv)

    loads[1].wait()
    loads[2].wait()

    def own_state(c):
        for i in range(2):
            f_own[c, pl.ds(i * dh, dh), :] = dot_tn(
                k[2 * c + i] * tail[...], v[2 * c + i]
            ).astype(BF)
        ahead.send(0, c)
        ahead.send(1, c)

    loop(pairs, own_state)
    loads[3].wait()

    def local_attention(head):
        scores[head] = dot_nt(q[head], k[head]).astype(BF) * mask[...]
        attn[head] = dot_nn(scores[head], v[head])

    loop(pairs, local_attention)
    p_mate.wait_recv()
    p_across.start()
    p_core.start()
    loop(pairs, ahead.first)
    loop(pairs, lambda i: local_attention(i + pairs))

    loads[4].wait()
    g_core.wait_recv()

    def cotangents(pair, slot):
        return dot_nt(
            g[slot],
            w[pl.ds(pl.multiple_of(pair * tile, tile), tile), pl.ds(pl.multiple_of(slot * share, 128), share)],
        )

    def first_cotangents(pair):
        gn[pair] = cotangents(pair, h) + cotangents(pair, core)

    loop(pairs, first_cotangents)

    reads[...] = ahead.reached()

    def nt_copy(c):
        at = pl.ds(pl.multiple_of(c * rows, rows), rows)
        return remote(nt.at[at, :], ntp.at[at, :], n_send.at[c], n_recv.at[c], mate, h)

    def scale_of(value):
        return lax.rsqrt(jnp.mean(value * value, axis=-1, keepdims=True) + 1e-05)

    def normalise(c):
        ahead.second(c, f_low)
        for i in range(2):
            head = 2 * c + i
            value = attn[head] + reads[...] * dot_nn(q[head], f_low[head])
            attn[head] = value
            low = (value * scale_of(value)).astype(BF)
            at = pl.ds(pl.multiple_of(head * dh, dh), dh)
            normed[:, at] = low
            nt[at, :] = low.T
        nt_copy(c).start()

    loop(pairs, normalise)

    g_across.wait_recv()
    g_pass.start()
    g_pass.wait_recv()

    def grad_attention(c):
        pair_gn = gn[c] + cotangents(c, across) + cotangents(c, both)
        for i in range(2):
            head = 2 * c + i
            value = attn[head]
            scale = scale_of(value)
            norm = value * scale
            grad = pair_gn[:, i * dh : (i + 1) * dh]
            low = (scale * (grad - norm * jnp.mean(grad * norm, axis=-1, keepdims=True))).astype(BF)
            ga[head] = low
            r_own[c, pl.ds(i * dh, dh), :] = dot_tn(q[head] * front[...], low).astype(BF)
        behind.send(0, c)
        behind.send(1, c)

    loop(pairs, grad_attention)
    p_across.wait_recv()
    p_pass.start()
    p_core.wait_recv()
    p_pass.wait_recv()

    def u_copy(d, j):
        at = pl.ds(pl.multiple_of(j * rows, rows), rows)
        return remote(sb.at[d, at, :], ub.at[d, at, :], u_ss.at[d, j], u_rs.at[d, j], s + 2, h)

    def d_copy(d, j):
        at = pl.ds(pl.multiple_of(j * rows, rows), rows)
        return remote(sb.at[d, at, :], db.at[d, at, :], d_ss.at[d, j], d_rs.at[d, j], s - 2, h)

    def weight_terms(j):
        nt_copy(j).wait_recv()
        at = pl.ds(pl.multiple_of(j * rows, rows), rows)

        def one(i):
            d = jnp.where(i % 2 == 0, line - 1 - i // 2, i // 2)
            d = jnp.where(a < line // 2, d, line - 1 - d)
            mine = g[d, :, pl.ds(pl.multiple_of(b * width, 128), width)]
            part[...] = dot_nn(nt[at, :], mine) + dot_nn(ntp[at, :], p[d])

            @pl.when((d > a) & (a > 0))
            def _():
                u_copy(d, j).wait_recv()
                part[...] += ub[d, at, :].astype(F32)

            @pl.when((d < a) & (a < line - 1))
            def _():
                d_copy(d, j).wait_recv()
                part[...] += db[d, at, :].astype(F32)

            @pl.when(d == a)
            def _():
                gacc[at, :] = part[...]

            @pl.when(d != a)
            def _():
                sb[d, at, :] = part[...].astype(BF)

            @pl.when(d > a)
            def _():
                u_copy(d, j).start()

            @pl.when(d < a)
            def _():
                d_copy(d, j).start()

        loop(line, one)

    weight_terms(0)

    tiles = share // tile

    def projected(d, t):
        at = pl.ds(pl.multiple_of(d * share + t * tile, 128), tile)
        return dot_nn(normed[...], w[:, at])

    def lc_copy(side):
        return remote(
            lc_send.at[side], lc_recv.at[side], lc_ss.at[side], lc_rs.at[side], s, core
        )

    lx_copy = remote(lx_send, lx_recv, lx_ss.at[0], lx_rs.at[0], s, across)

    def columns(t):
        return pl.ds(pl.multiple_of(t * tile, tile), tile)

    for side in (1 - hx, hx):
        def give(t, side=side):
            lc_send[side, :, columns(t)] = projected(2 * side + 1 - hc, t).astype(BF)

        loop(tiles, give)
        lc_copy(side).start()

    loop(pairs, behind.first)

    lc_copy(1 - hx).wait_recv()

    def cross(t):
        lx_send[:, columns(t)] = (
            projected(2 * (1 - hx) + hc, t) + lc_recv[1 - hx, :, columns(t)].astype(F32)
        ).astype(BF)

    loop(tiles, cross)
    lx_copy.start()
    weight_terms(1)

    lc_copy(hx).wait_recv()

    def keep(t):
        lo_acc[:, columns(t)] = projected(h, t) + lc_recv[hx, :, columns(t)].astype(F32)

    loop(tiles, keep)

    loop(pairs, lambda c: behind.second(c, r_low))
    writes[...] = behind.reached()

    def out_copy(src, dst, i):
        return pltpu.make_async_copy(src, dst, out_sem.at[i])

    def backward(head):
        grad = ga[head]
        gs = dot_nt(grad, v[head]).astype(BF) * mask[...]
        gq[head] = (
            dot_nn(gs, k[head]) + reads[...] * dot_nt(grad, f_low[head])
        ).astype(BF)
        gk[head] = (
            dot_tn(gs, q[head]) + writes[...] * dot_nt(v[head], r_low[head])
        ).astype(BF)
        gv[head] = (
            dot_tn(scores[head], grad) + writes[...] * dot_nn(k[head], r_low[head])
        ).astype(BF)

    loop(pairs, backward)
    weight_terms(2)
    loop(pairs, lambda i: backward(i + pairs))
    outs = [out_copy(gq, gq_out, 0), out_copy(gk, gk_out, 1), out_copy(gv, gv_out, 2)]
    for copy in outs:
        copy.start()
    weight_terms(3)

    lx_copy.wait_recv()
    lo_fin[...] = (lo_acc[...] + lx_recv[...].astype(F32)).astype(BF)
    outs.append(out_copy(lo_fin, lo_out, 3))
    outs[-1].start()

    def finish(j):
        at = pl.ds(pl.multiple_of(j * rows, rows), rows)

        @pl.when(a > 0)
        def _():
            u_copy(a, j).wait_recv()
            gacc[at, :] += ub[a, at, :].astype(F32)

        @pl.when(a < line - 1)
        def _():
            d_copy(a, j).wait_recv()
            gacc[at, :] += db[a, at, :].astype(F32)

    loop(pairs, finish)
    outs.append(out_copy(gacc, gw_out, 4))
    outs[-1].start()

    for copy in (g_core, g_across, g_pass, p_mate, p_core, p_across, p_pass, lx_copy):
        copy.wait_send()
    for side in range(2):
        lc_copy(side).wait_send()

    def drain(c):
        nt_copy(c).wait_send()
        for kind in range(3):
            ahead.sent(kind, c)
            behind.sent(kind, c)

        def lines(d):
            @pl.when(d > a)
            def _():
                u_copy(d, c).wait_send()

            @pl.when(d < a)
            def _():
                d_copy(d, c).wait_send()

        loop(line, lines)

    loop(pairs, drain)
    for copy in outs:
        copy.wait()


def fused(queries, key_vectors, value_vectors, doc_ids, out_weight, grad_out):
    n = lax.axis_size("seq")
    m = lax.axis_size("head")
    length, heads, dh = queries.shape
    feats, columns = out_weight.shape
    share = columns // m
    width = columns // n
    line = n // 2
    pairs = heads // 2
    by_head = [x.transpose(1, 0, 2) for x in (queries, key_vectors, value_vectors)]
    docs = doc_ids.reshape(1, length)
    vm = pltpu.VMEM
    heads_bf = vm((heads, length, dh), BF)
    state = vm((pairs, 2 * dh + 16, dh), BF)
    low = vm((heads, dh, dh), BF)
    terms = vm((line, feats, width), BF)
    dma = pltpu.SemaphoreType.DMA
    scratch = [
        heads_bf, heads_bf, heads_bf,
        vm((feats, columns), BF),
        vm((m, length, share), BF),
        vm((m, length, width), BF),
        vm((length, length), BF),
        vm((heads, length, length), BF),
        vm((heads, length, dh), F32),
        vm((pairs, length, 2 * dh), F32),
        vm((length, feats), BF),
        vm((feats, length), BF),
        vm((feats, length), BF),
        heads_bf,
        state, state, state, state, state, low,
        state, state, state, state, state, low,
        vm((2, length, share), BF), vm((2, length, share), BF),
        vm((length, share), BF), vm((length, share), BF),
        vm((length, share), F32), vm((length, share), BF),
        terms, terms, terms,
        vm((feats, width), F32), vm((2 * dh, width), F32),
        heads_bf, heads_bf, heads_bf,
        vm((length, dh), F32), vm((length, dh), F32), vm((length, dh), F32),
        vm((length, dh), BF), vm((length, dh), BF),
        dma((5,)), dma((3,)), dma((3,)), dma((4,)), dma((4,)),
        dma((3, pairs)), dma((3, pairs)), dma((3, pairs)), dma((3, pairs)),
        dma((pairs,)), dma((pairs,)), dma((2,)), dma((2,)), dma((1,)), dma((1,)),
        dma((line, pairs)), dma((line, pairs)), dma((line, pairs)), dma((line, pairs)),
        dma((5,)),
    ]
    anywhere = pl.BlockSpec(memory_space=pl.ANY)
    grads = jax.ShapeDtypeStruct((heads, length, dh), BF)
    lo, gq, gk, gv, gw = pl.pallas_call(
        functools.partial(kernel, (n, m, heads, length, dh, share, width)),
        out_shape=(
            jax.ShapeDtypeStruct((length, share), BF), grads, grads, grads,
            jax.ShapeDtypeStruct((feats, width), F32),
        ),
        in_specs=[pl.BlockSpec(memory_space=pltpu.VMEM)] + [anywhere] * 5,
        out_specs=(anywhere,) * 5,
        scratch_shapes=scratch,
        compiler_params=pltpu.CompilerParams(
            collective_id=0, has_side_effects=True, vmem_limit_bytes=60 << 20
        ),
    )(docs, *by_head, out_weight, grad_out)
    return (lo, gq.transpose(1, 0, 2), gk.transpose(1, 0, 2), gv.transpose(1, 0, 2), gw)


def shift(block, distance):
    n = lax.axis_size("seq")
    route = [(i, i + distance) for i in range(n) if 0 <= i + distance < n]
    return lax.ppermute(block, "seq", route)


def swap(block, axis, bit):
    n = lax.axis_size(axis)
    return lax.ppermute(block, axis, [(i, i ^ bit) for i in range(n)])


def gather_heads(block, first):
    me = lax.axis_index("head")
    bit = lax.axis_size("head") // 2
    columns = block.shape[1]
    held = [block]
    while bit:
        other = swap(jnp.concatenate(held, axis=1), "head", bit)
        if first is not None:
            other, first = lax.optimization_barrier((other, first))
            first = None
        high = (me // bit) % 2 == 1
        merged = []
        for i, own in enumerate(held):
            theirs = other[:, i * columns : (i + 1) * columns]
            merged += [jnp.where(high, theirs, own), jnp.where(high, own, theirs)]
        held = merged
        bit //= 2
    return held


def scatter_heads(partial):
    me = lax.axis_index("head")
    size = lax.axis_size("head")
    share = partial.shape[1] // size
    held = [partial[:, i * share : (i + 1) * share] for i in range(size)]
    bit = 1
    while bit < size:
        high = (me // bit) % 2 == 1
        couples = list(zip(held[0::2], held[1::2]))
        given = jnp.concatenate([jnp.where(high, a, b).astype(BF) for a, b in couples], axis=1)
        other = swap(given, "head", bit)
        held = [
            jnp.where(high, b, a) + other[:, i * share : (i + 1) * share].astype(F32)
            for i, (a, b) in enumerate(couples)
        ]
        bit *= 2
    return held[0].astype(BF)


def with_doc(state, doc):
    rows = jnp.broadcast_to(doc.astype(BF)[:, None], (16, state.shape[-1]))
    return jnp.concatenate([state.astype(BF).reshape(-1, state.shape[-1]), rows], axis=0)


def window(total, sign, first=None):
    rows = lax.broadcasted_iota(jnp.int32, (total.shape[0], 1), 0) < total.shape[0] - 16
    span = 1
    while span < lax.axis_size("seq") // 2:
        far = shift(total, sign * span)
        if first is not None and 4 * span >= lax.axis_size("seq"):
            far, first = lax.optimization_barrier((far, first))
        same = (far[-16:-15] == total[-16:-15]) & rows
        total = total + jnp.where(same, far, jnp.zeros_like(far))
        span *= 2
    return total


def plain(queries, key_vectors, value_vectors, doc_ids, out_weight, grad_out):
    n = lax.axis_size("seq")
    m = lax.axis_size("head")
    length, heads, dh = queries.shape
    place = lax.axis_index("seq")
    parity = place % 2
    line = n // 2
    where_on_line = place // 2
    columns = out_weight.shape[1]
    width = columns // n

    docs = doc_ids.astype(F32)
    tail = (docs == docs[-1]).astype(BF)
    own_state = jnp.einsum(
        "shd,she->hde", key_vectors * tail[:, None, None], value_vectors, preferred_element_type=F32
    )
    near_flat = shift(with_doc(own_state, docs[-1:]), 1)
    own_gathered = gather_heads(grad_out, near_flat)
    near_flat, grad_out = lax.optimization_barrier((near_flat, grad_out))
    flat = window(near_flat, 1)
    before = flat[-16, :1].astype(F32)
    state_low = flat[:-16].reshape(own_state.shape)

    causal = lax.broadcasted_iota(jnp.int32, (length, length), 0) >= lax.broadcasted_iota(
        jnp.int32, (length, length), 1
    )
    pairs = causal & (docs[:, None] == docs[None, :])
    reads = (docs == before[0]).astype(F32)
    scores = jnp.einsum("thd,shd->hts", queries, key_vectors, preferred_element_type=F32)
    scores_low = jnp.where(pairs[None], scores, 0.0).astype(BF)
    attn = jnp.einsum("hts,she->the", scores_low, value_vectors, preferred_element_type=F32)
    attn = attn + reads[:, None, None] * jnp.einsum(
        "thd,hde->the", queries, state_low, preferred_element_type=F32
    )
    scale = lax.rsqrt(jnp.mean(attn * attn, axis=-1, keepdims=True) + 1e-05)
    normed_f = attn * scale
    normed = normed_f.astype(BF).reshape(length, -1)
    partner_normed = swap(normed, "seq", 1)

    share = columns // m
    odd = parity == 1
    for_partner = [
        jnp.where(odd, grad_out[:, i : i + width], grad_out[:, i + width : i + 2 * width])
        for i in range(0, share, 2 * width)
    ]
    from_partner = swap(jnp.concatenate(for_partner, axis=1), "seq", 1)
    cotangent = jnp.concatenate(own_gathered, axis=1)
    partner_cot = jnp.concatenate(gather_heads(from_partner, normed), axis=1)

    grad_normed = lax.dot_general(
        cotangent, out_weight, (((1,), (1,)), ((), ())), preferred_element_type=F32
    ).reshape(attn.shape)
    grad_attn = (
        scale * (grad_normed - normed_f * jnp.mean(grad_normed * normed_f, axis=-1, keepdims=True))
    ).astype(BF)
    head_mask = (docs == docs[0]).astype(BF)
    own_back = jnp.einsum(
        "thd,the->hde", queries * head_mask[:, None, None], grad_attn, preferred_element_type=F32
    )
    near_flat = shift(with_doc(own_back, docs[:1]), -1)

    def share_of(step):
        goal = (where_on_line + step) % line
        mine = lax.dynamic_slice_in_dim(cotangent, (2 * goal + parity) * width, width, 1)
        theirs = lax.dynamic_slice_in_dim(partner_cot, goal * width, width, 1)
        over_tokens = (((0,), (0,)), ((), ()))
        return lax.dot_general(
            normed, mine, over_tokens, preferred_element_type=F32
        ) + lax.dot_general(partner_normed, theirs, over_tokens, preferred_element_type=F32)

    terms = [share_of(step).astype(BF) for step in range(1, line)]
    terms, near_flat = lax.optimization_barrier((terms, near_flat))
    terms, grad_attn_in, normed_out = lax.optimization_barrier((terms, grad_attn, normed))
    partial_out = jnp.dot(normed_out, out_weight, preferred_element_type=F32)
    layer_out = scatter_heads(partial_out)
    flat = window(near_flat, -1, layer_out)
    after = flat[-16, :1].astype(F32)
    back_low = flat[:-16].reshape(own_back.shape)
    writes = (docs == after[0]).astype(F32)
    arrived = []
    for step, term in enumerate(terms, 1):
        route = [
            (2 * a + b, 2 * ((a + step) % line) + b) for a in range(line) for b in range(2)
        ]
        arrived.append(lax.ppermute(term, "seq", route))
    own_term = share_of(0)

    grad_scores = jnp.einsum("the,she->hts", grad_attn_in, value_vectors, preferred_element_type=F32)
    grad_scores = jnp.where(pairs[None], grad_scores, 0.0).astype(BF)
    grad_queries = jnp.einsum("hts,shd->thd", grad_scores, key_vectors, preferred_element_type=F32)
    grad_queries = grad_queries + reads[:, None, None] * jnp.einsum(
        "the,hde->thd", grad_attn_in, state_low, preferred_element_type=F32
    )
    grad_keys = jnp.einsum("hts,thd->shd", grad_scores, queries, preferred_element_type=F32)
    grad_keys = grad_keys + writes[:, None, None] * jnp.einsum(
        "she,hde->shd", value_vectors, back_low, preferred_element_type=F32
    )
    grad_values = jnp.einsum("hts,the->she", scores_low, grad_attn_in, preferred_element_type=F32)
    grad_values = grad_values + writes[:, None, None] * jnp.einsum(
        "shd,hde->she", key_vectors, back_low, preferred_element_type=F32
    )
    arrived, layer_out = lax.optimization_barrier((arrived, layer_out))
    grad_weight = own_term
    for part in arrived:
        grad_weight = grad_weight + part.astype(F32)
    return (
        layer_out,
        grad_queries.astype(BF),
        grad_keys.astype(BF),
        grad_values.astype(BF),
        grad_weight,
    )


def fits(mesh, columns, heads, dh):
    n, m = mesh.shape["seq"], mesh.shape["head"]
    return m == 4 and n == 2 * m and columns % (128 * n) == 0 and heads == 8 and dh == 128


def choose(mesh):
    def shards(queries, key_vectors, value_vectors, doc_ids, out_weight, grad_out):
        heads, dh = queries.shape[1:]
        form = fused if fits(mesh, out_weight.shape[1], heads, dh) else plain
        return form(queries, key_vectors, value_vectors, doc_ids, out_weight, grad_out)

    return shards


def solution(mesh):
    placed = (
        P("seq", "head", None),
        P("seq", "head", None),
        P("seq", "head", None),
        P("seq"),
        P("head", None),
        P("seq", "head"),
    )
    return jax.shard_map(
        choose(mesh),
        mesh=mesh,
        in_specs=placed,
        out_specs=(
            P("seq", "head"),
            P("seq", "head", None),
            P("seq", "head", None),
            P("seq", "head", None),
            P("head", "seq"),
        ),
        check_vma=False,
    )
```

```python
import functools

import jax
import jax.numpy as jnp
from jax import lax
from jax.experimental import pallas as pl
from jax.experimental.pallas import tpu as pltpu
from jax.sharding import PartitionSpec as P


BF = jnp.bfloat16
F32 = jnp.float32
MESH = pl.DeviceIdType.MESH


def dot_nn(a, b):
    return lax.dot_general(a, b, (((1,), (0,)), ((), ())), preferred_element_type=F32)


def dot_nt(a, b):
    return lax.dot_general(a, b, (((1,), (1,)), ((), ())), preferred_element_type=F32)


def dot_tn(a, b):
    return lax.dot_general(a, b, (((0,), (0,)), ((), ())), preferred_element_type=F32)


def loop(count, body):
    lax.fori_loop(0, count, lambda i, _: (body(i), None)[1], None)


def kernel(
    sizes,
    docs_ref, q_hbm, k_hbm, v_hbm, w_hbm, go_hbm,
    lo_out, gq_out, gk_out, gv_out, gw_out,
    raw_q, raw_k, raw_v, q, k, v, w, g, p, mask, scores, attn, gn, normed, nt, ntp, ga,
    f_own, f_mate, f_next, f_carry, f_low,
    r_own, r_mate, r_next, r_carry, r_low,
    lc_send, lc_recv, lx_send, lx_recv, lo_acc, lo_fin,
    sb, ub, db, gacc, part,
    doc_col, reads, writes, tail, front,
    in_sem, g_send, g_recv, p_send, p_recv, f_send, f_recv, r_send, r_recv,
    n_send, n_recv, lc_ss, lc_rs, lx_ss, lx_rs, u_ss, u_rs, d_ss, d_rs, out_sem,
):
    n, m, heads, length, dh, share, width = sizes
    line = n // 2
    pairs = heads // 2
    rows = 2 * dh
    tile = 2 * dh
    s = lax.axis_index("seq")
    h = lax.axis_index("head")
    a = s // 2
    b = s % 2
    hc = h % 2
    hx = h // 2
    core = h + 1 - 2 * hc
    across = h + 2 - 4 * hx
    both = core + 2 - 4 * hx
    mate = s + 1 - 2 * b
    at_end = (a == 0) | (a == line - 1)

    barrier = pltpu.get_barrier_semaphore()

    def greet(seq, head):
        pl.semaphore_signal(barrier, inc=1, device_id=(seq, head), device_id_type=MESH)

    def local(src, dst, i):
        return pltpu.make_async_copy(src, dst, in_sem.at[i])

    def remote(src, dst, ss, rs, seq, head):
        return pltpu.make_async_remote_copy(
            src_ref=src, dst_ref=dst, send_sem=ss, recv_sem=rs,
            device_id=(seq, head), device_id_type=MESH,
        )

    loads = [
        local(go_hbm, g.at[h], 0), local(k_hbm, raw_k, 1), local(v_hbm, raw_v, 2),
        local(q_hbm, raw_q, 3), local(w_hbm, w, 4),
    ]
    for copy in loads:
        copy.start()
    greet(s, core)
    greet(s, across)
    greet(mate, h)

    @pl.when(a < line - 1)
    def _():
        greet(s + 2, h)

    @pl.when(a > 0)
    def _():
        greet(s - 2, h)

    def spot(cond):
        return jnp.where(cond, 1, 0)

    docs_row = docs_ref[...].astype(F32)
    doc_col[...] = jnp.broadcast_to(docs_row, (dh, length)).T
    last_doc = doc_col[pl.ds(length - 1, 1), :]
    first_doc = doc_col[pl.ds(0, 1), :]
    tail[...] = jnp.where(doc_col[...] == last_doc, 1.0, 0.0).astype(BF)
    front[...] = jnp.where(doc_col[...] == first_doc, 1.0, 0.0).astype(BF)
    for c in range(pairs):
        f_own[c, pl.ds(rows, 16), :] = jnp.broadcast_to(last_doc, (16, dh)).astype(BF)
        r_own[c, pl.ds(rows, 16), :] = jnp.broadcast_to(first_doc, (16, dh)).astype(BF)

    def blank(ref):
        ref[...] = jnp.zeros_like(ref)
        for c in range(pairs):
            ref[c, pl.ds(rows, 16), :] = jnp.full((16, dh), -1.0, BF)

    @pl.when(a == 0)
    def _():
        blank(f_carry)

    @pl.when(a == line - 1)
    def _():
        blank(r_carry)

    pl.semaphore_wait(barrier, 3 + spot(a < line - 1) + spot(a > 0))

    loads[0].wait()
    theirs = pl.ds(pl.multiple_of((1 - b) * width, 128), width)
    ours = pl.ds(pl.multiple_of(b * width, 128), width)

    def g_part(slot, at, i, to):
        part_of = g.at[slot, at[0], at[1]]
        return remote(part_of, part_of, g_send.at[i], g_recv.at[i], s, to)

    whole = pl.ds(0, length)
    upper, under = pl.ds(0, length // 2), pl.ds(length // 2, length // 2)
    g_core = g_part(h, (whole, pl.ds(0, share)), 0, core)
    g_ours = g_part(h, (whole, ours), 1, across)
    g_upper = g_part(h, (upper, theirs), 2, across)
    g_under = g_part(h, (under, theirs), 3, across)
    g_pass_ours = g_part(across, (whole, ours), 4, core)
    g_pass_theirs = g_part(across, (whole, theirs), 5, core)
    p_mate = remote(g.at[h, :, theirs], p.at[h], p_send.at[0], p_recv.at[0], mate, h)
    p_across = remote(p.at[h], p.at[h], p_send.at[1], p_recv.at[1], s, across)
    p_core = remote(p.at[h], p.at[h], p_send.at[2], p_recv.at[2], s, core)
    p_pass = remote(p.at[across], p.at[across], p_send.at[3], p_recv.at[3], s, core)
    g_ours.start()
    g_upper.start()
    g_core.start()

    class States:
        def __init__(self, sign, step, odd, own, mate_ref, after, carry, low, ss, rs):
            self.sign, self.step, self.odd = sign, step, odd
            self.own, self.mate, self.after, self.carry, self.low = own, mate_ref, after, carry, low
            self.ss, self.rs = ss, rs

        def swap(self, c):
            return remote(
                self.own.at[c], self.mate.at[c], self.ss.at[0, c], self.rs.at[0, c], mate, h
            )

        def onward(self, c):
            return remote(
                self.after.at[c], self.carry.at[c], self.ss.at[1, c], self.rs.at[1, c],
                s + self.sign * 2, h,
            )

        def values(self, ref, c):
            return (
                ref[c, pl.ds(0, rows), :].astype(F32),
                ref[c, pl.ds(rows, 1), :].astype(F32),
            )

        def add(self, base, more):
            same = jnp.broadcast_to(jnp.where(base[1] == more[1], 1.0, 0.0), (rows, dh))
            return base[0] + more[0] * same, base[1]

        def members(self, c):
            mine, other = self.values(self.own, c), self.values(self.mate, c)
            odd = self.odd == 1
            early = tuple(jnp.where(odd, y, x) for x, y in zip(mine, other))
            late = tuple(jnp.where(odd, x, y) for x, y in zip(mine, other))
            return early, late

        def forward(self, c):
            early, late = self.members(c)
            total, doc = self.add(self.add(late, early), self.values(self.carry, c))
            self.after[c, pl.ds(0, rows), :] = total.astype(BF)
            self.after[c, pl.ds(rows, 16), :] = jnp.broadcast_to(doc, (16, dh)).astype(BF)
            self.onward(c).start()

        def settle(self, c):
            early, _ = self.members(c)
            carry = self.values(self.carry, c)
            odd = self.odd == 1
            total = jnp.where(odd, self.add(early, carry)[0], carry[0]).astype(BF)
            self.low[2 * c] = total[:dh]
            self.low[2 * c + 1] = total[dh:]

        def open(self, c):
            self.swap(c).wait_recv()

            @pl.when(self.step == 0)
            def _():
                self.forward(c)

        def serve(self, c):
            @pl.when((self.step > 0) & (c > 0))
            def _():
                self.onward(c).wait_recv()

            @pl.when((self.step > 0) & (self.step < line - 1))
            def _():
                self.forward(c)

            self.settle(c)

        def reached(self):
            early, _ = self.members(0)
            doc = jnp.where(self.odd == 1, early[1], self.values(self.carry, 0)[1])
            return jnp.where(doc_col[...] == doc, 1.0, 0.0)

        def drain(self, c):
            self.swap(c).wait_send()

            @pl.when(self.step < line - 1)
            def _():
                self.onward(c).wait_send()

    ahead = States(1, a, b, f_own, f_mate, f_next, f_carry, f_low, f_send, f_recv)
    behind = States(
        -1, line - 1 - a, 1 - b, r_own, r_mate, r_next, r_carry, r_low, r_send, r_recv
    )

    some = 64

    def by_head(raw, ref):
        def block(i):
            at = pl.ds(pl.multiple_of(i * some, some), some)
            ref[:, at, :] = jnp.swapaxes(raw[at], 0, 1)

        loop(length // some, block)

    def by_token(ref, raw):
        def block(i):
            at = pl.ds(pl.multiple_of(i * some, some), some)
            raw[at] = jnp.swapaxes(ref[:, at, :], 0, 1)

        loop(length // some, block)

    loads[1].wait()
    by_head(raw_k, k)
    loads[2].wait()
    by_head(raw_v, v)

    def own_state(c):
        for i in range(2):
            f_own[c, pl.ds(i * dh, dh), :] = dot_tn(
                k[2 * c + i] * tail[...], v[2 * c + i]
            ).astype(BF)
        ahead.swap(c).start()

    own_state(0)
    p_mate.start()
    loop(pairs - 1, lambda c: own_state(c + 1))
    loads[3].wait()
    by_head(raw_q, q)

    for i in range(length // dh):
        at = pl.ds(i * dh, dh)
        col = doc_col[at, :][:, :1]
        t_pos = lax.broadcasted_iota(jnp.int32, (dh, length), 0) + i * dh
        s_pos = lax.broadcasted_iota(jnp.int32, (dh, length), 1)
        ok = (t_pos >= s_pos) & (col == docs_row)
        mask[at, :] = jnp.where(ok, 1.0, 0.0).astype(BF)

    ahead.open(0)

    def local_attention(head):
        scores[head] = dot_nt(q[head], k[head]).astype(BF) * mask[...]
        attn[head] = dot_nn(scores[head], v[head])

    def between(low, high, body):
        lax.fori_loop(low, high, lambda i, _: (body(i), None)[1], None)

    def cotangents(pair, slot):
        return dot_nt(
            g[slot],
            w[pl.ds(pl.multiple_of(pair * tile, tile), tile), pl.ds(pl.multiple_of(slot * share, 128), share)],
        )

    def first_cotangents(pair):
        gn[pair] = cotangents(pair, h) + cotangents(pair, core)

    def hand_on():
        p_mate.wait_recv()
        p_across.start()
        p_core.start()
        g_under.start()
        g_ours.wait_recv()
        g_pass_ours.start()
        loads[4].wait()
        g_core.wait_recv()
        loop(pairs, first_cotangents)

    def nt_copy(head):
        at = pl.ds(pl.multiple_of(head * dh, dh), dh)
        return remote(nt.at[at, :], ntp.at[at, :], n_send.at[head], n_recv.at[head], mate, h)

    def scale_of(value):
        return lax.rsqrt(jnp.mean(value * value, axis=-1, keepdims=True) + 1e-05)

    def normalise(c):
        ahead.serve(c)
        for i in range(2):
            head = 2 * c + i
            value = attn[head] + reads[...] * dot_nn(q[head], f_low[head])
            attn[head] = value
            low = (value * scale_of(value)).astype(BF)
            at = pl.ds(pl.multiple_of(head * dh, dh), dh)
            normed[:, at] = low
            nt[at, :] = low.T

            @pl.when(c < pairs // 2)
            def _():
                nt_copy(head).start()

    late = a >= line // 2
    enough = jnp.where(late, heads, heads // 2)
    between(0, enough, local_attention)

    @pl.when(late)
    def _():
        hand_on()

    @pl.when(a > 0)
    def _():
        ahead.onward(0).wait_recv()

    reads[...] = ahead.reached()
    normalise(0)
    between(enough, heads, local_attention)

    @pl.when(~late)
    def _():
        hand_on()

    loop(pairs - 1, lambda c: ahead.open(c + 1))
    between(1, jnp.where(at_end, 1, pairs), normalise)

    p_across.wait_recv()
    p_pass.start()
    p_core.wait_recv()
    g_pass_ours.wait_recv()
    p_pass.wait_recv()

    def u_copy(d, j):
        at = pl.ds(pl.multiple_of(j * rows, rows), rows)
        return remote(sb.at[d, at, :], ub.at[d, at, :], u_ss.at[d, j], u_rs.at[d, j], s + 2, h)

    def d_copy(d, j):
        at = pl.ds(pl.multiple_of(j * rows, rows), rows)
        return remote(sb.at[d, at, :], db.at[d, at, :], d_ss.at[d, j], d_rs.at[d, j], s - 2, h)

    def weight_terms(j):
        nt_copy(2 * j).wait_recv()
        nt_copy(2 * j + 1).wait_recv()
        at = pl.ds(pl.multiple_of(j * rows, rows), rows)

        def one(i):
            d = jnp.where(i % 2 == 0, line - 1 - i // 2, i // 2)
            d = jnp.where(a < line // 2, d, line - 1 - d)
            part[...] = dot_nn(nt[at, :], g[d, :, ours]) + dot_nn(ntp[at, :], p[d])

            @pl.when((d > a) & (a > 0))
            def _():
                u_copy(d, j).wait_recv()
                part[...] += ub[d, at, :].astype(F32)

            @pl.when((d < a) & (a < line - 1))
            def _():
                d_copy(d, j).wait_recv()
                part[...] += db[d, at, :].astype(F32)

            @pl.when(d == a)
            def _():
                gacc[at, :] = part[...]

            @pl.when(d != a)
            def _():
                sb[d, at, :] = part[...].astype(BF)

            @pl.when(d > a)
            def _():
                u_copy(d, j).start()

            @pl.when(d < a)
            def _():
                d_copy(d, j).start()

        loop(line, one)

    weight_terms(0)
    between(jnp.where(at_end, 1, pairs), pairs, normalise)
    g_upper.wait_recv()
    g_under.wait_recv()
    g_pass_theirs.start()
    g_pass_theirs.wait_recv()

    def grad_attention(c):
        pair_gn = gn[c] + cotangents(c, across) + cotangents(c, both)
        for i in range(2):
            head = 2 * c + i
            value = attn[head]
            scale = scale_of(value)
            norm = value * scale
            grad = pair_gn[:, i * dh : (i + 1) * dh]
            low = (scale * (grad - norm * jnp.mean(grad * norm, axis=-1, keepdims=True))).astype(BF)
            ga[head] = low
            r_own[c, pl.ds(i * dh, dh), :] = dot_tn(q[head] * front[...], low).astype(BF)
        behind.swap(c).start()

    loop(pairs, grad_attention)
    between(heads // 2, heads, lambda head: nt_copy(head).start())

    @pl.when(at_end)
    def _():
        weight_terms(1)

    tiles = share // tile

    def projected(d, t):
        at = pl.ds(pl.multiple_of(d * share + t * tile, 128), tile)
        return dot_nn(normed[...], w[:, at])

    def lc_copy(side):
        return remote(
            lc_send.at[side], lc_recv.at[side], lc_ss.at[side], lc_rs.at[side], s, core
        )

    lx_copy = remote(lx_send, lx_recv, lx_ss.at[0], lx_rs.at[0], s, across)

    def columns(t):
        return pl.ds(pl.multiple_of(t * tile, tile), tile)

    for side in (1 - hx, hx):
        def give(t, side=side):
            lc_send[side, :, columns(t)] = projected(2 * side + 1 - hc, t).astype(BF)

        loop(tiles, give)
        lc_copy(side).start()

    loop(pairs, behind.open)
    lc_copy(1 - hx).wait_recv()

    def cross(t):
        lx_send[:, columns(t)] = (
            projected(2 * (1 - hx) + hc, t) + lc_recv[1 - hx, :, columns(t)].astype(F32)
        ).astype(BF)

    loop(tiles, cross)
    lx_copy.start()

    @pl.when(~at_end)
    def _():
        weight_terms(1)

    @pl.when(at_end)
    def _():
        weight_terms(2)

    def backward(c):
        for i in range(2):
            head = 2 * c + i
            grad = ga[head]
            gs = dot_nt(grad, v[head]).astype(BF) * mask[...]
            gq = dot_nn(gs, k[head]) + reads[...] * dot_nt(grad, f_low[head])
            attn[head] = dot_tn(gs, q[head])
            gn[c, :, pl.ds(i * dh, dh)] = dot_tn(scores[head], grad)
            q[head] = gq.astype(BF)

    loop(pairs, backward)

    @pl.when(at_end)
    def _():
        between(3, pairs, weight_terms)

    lc_copy(hx).wait_recv()

    def keep(t):
        lo_acc[:, columns(t)] = projected(h, t) + lc_recv[hx, :, columns(t)].astype(F32)

    loop(tiles, keep)

    def out_copy(src, dst, i):
        return pltpu.make_async_copy(src, dst, out_sem.at[i])

    outs = []

    def give_back(ref, raw, out, i):
        by_token(ref, raw)
        outs.append(out_copy(raw, out, i))
        outs[-1].start()

    give_back(q, raw_q, gq_out, 0)

    @pl.when(behind.step > 0)
    def _():
        behind.onward(0).wait_recv()

    writes[...] = behind.reached()
    loop(pairs, behind.serve)

    def backward_states(c):
        for i in range(2):
            head = 2 * c + i
            gk = attn[head] + writes[...] * dot_nt(v[head], r_low[head])
            gv = gn[c, :, pl.ds(i * dh, dh)] + writes[...] * dot_nn(k[head], r_low[head])
            k[head] = gk.astype(BF)
            v[head] = gv.astype(BF)

    loop(pairs, backward_states)
    give_back(k, raw_k, gk_out, 1)
    give_back(v, raw_v, gv_out, 2)

    @pl.when(~at_end)
    def _():
        between(2, pairs, weight_terms)

    lx_copy.wait_recv()
    lo_fin[...] = (lo_acc[...] + lx_recv[...].astype(F32)).astype(BF)
    outs.append(out_copy(lo_fin, lo_out, 3))
    outs[-1].start()

    def finish(j):
        at = pl.ds(pl.multiple_of(j * rows, rows), rows)

        @pl.when(a > 0)
        def _():
            u_copy(a, j).wait_recv()
            gacc[at, :] += ub[a, at, :].astype(F32)

        @pl.when(a < line - 1)
        def _():
            d_copy(a, j).wait_recv()
            gacc[at, :] += db[a, at, :].astype(F32)

    loop(pairs, finish)
    outs.append(out_copy(gacc, gw_out, 4))
    outs[-1].start()

    for copy in (
        g_core, g_ours, g_upper, g_under, g_pass_ours, g_pass_theirs,
        p_mate, p_across, p_core, p_pass, lx_copy,
    ):
        copy.wait_send()
    for side in range(2):
        lc_copy(side).wait_send()

    def drain(c):
        nt_copy(2 * c).wait_send()
        nt_copy(2 * c + 1).wait_send()
        ahead.drain(c)
        behind.drain(c)

        def lines(d):
            @pl.when(d > a)
            def _():
                u_copy(d, c).wait_send()

            @pl.when(d < a)
            def _():
                d_copy(d, c).wait_send()

        loop(line, lines)

    loop(pairs, drain)
    for copy in outs:
        copy.wait()


def fused(queries, key_vectors, value_vectors, doc_ids, out_weight, grad_out):
    n = lax.axis_size("seq")
    m = lax.axis_size("head")
    length, heads, dh = queries.shape
    feats, columns = out_weight.shape
    share = columns // m
    width = columns // n
    line = n // 2
    pairs = heads // 2
    docs = doc_ids.reshape(1, length)
    vm = pltpu.VMEM
    heads_bf = vm((heads, length, dh), BF)
    state = vm((pairs, 2 * dh + 16, dh), BF)
    low = vm((heads, dh, dh), BF)
    terms = vm((line, feats, width), BF)
    dma = pltpu.SemaphoreType.DMA
    by_token = vm((length, heads, dh), BF)
    scratch = [
        by_token, by_token, by_token,
        heads_bf, heads_bf, heads_bf,
        vm((feats, columns), BF),
        vm((m, length, share), BF),
        vm((m, length, width), BF),
        vm((length, length), BF),
        vm((heads, length, length), BF),
        vm((heads, length, dh), F32),
        vm((pairs, length, 2 * dh), F32),
        vm((length, feats), BF),
        vm((feats, length), BF),
        vm((feats, length), BF),
        heads_bf,
        state, state, state, state, low,
        state, state, state, state, low,
        vm((2, length, share), BF), vm((2, length, share), BF),
        vm((length, share), BF), vm((length, share), BF),
        vm((length, share), F32), vm((length, share), BF),
        terms, terms, terms,
        vm((feats, width), F32), vm((2 * dh, width), F32),
        vm((length, dh), F32), vm((length, dh), F32), vm((length, dh), F32),
        vm((length, dh), BF), vm((length, dh), BF),
        dma((5,)), dma((6,)), dma((6,)), dma((4,)), dma((4,)),
        dma((2, pairs)), dma((2, pairs)), dma((2, pairs)), dma((2, pairs)),
        dma((heads,)), dma((heads,)), dma((2,)), dma((2,)), dma((1,)), dma((1,)),
        dma((line, pairs)), dma((line, pairs)), dma((line, pairs)), dma((line, pairs)),
        dma((5,)),
    ]
    anywhere = pl.BlockSpec(memory_space=pl.ANY)
    grads = jax.ShapeDtypeStruct((length, heads, dh), BF)
    lo, gq, gk, gv, gw = pl.pallas_call(
        functools.partial(kernel, (n, m, heads, length, dh, share, width)),
        out_shape=(
            jax.ShapeDtypeStruct((length, share), BF), grads, grads, grads,
            jax.ShapeDtypeStruct((feats, width), F32),
        ),
        in_specs=[pl.BlockSpec(memory_space=pltpu.VMEM)] + [anywhere] * 5,
        out_specs=(anywhere,) * 5,
        scratch_shapes=scratch,
        compiler_params=pltpu.CompilerParams(
            collective_id=0, has_side_effects=True, vmem_limit_bytes=60 << 20
        ),
    )(docs, queries, key_vectors, value_vectors, out_weight, grad_out)
    return lo, gq, gk, gv, gw


def shift(block, distance):
    n = lax.axis_size("seq")
    route = [(i, i + distance) for i in range(n) if 0 <= i + distance < n]
    return lax.ppermute(block, "seq", route)


def swap(block, axis, bit):
    n = lax.axis_size(axis)
    return lax.ppermute(block, axis, [(i, i ^ bit) for i in range(n)])


def gather_heads(block, first):
    me = lax.axis_index("head")
    bit = lax.axis_size("head") // 2
    columns = block.shape[1]
    held = [block]
    while bit:
        other = swap(jnp.concatenate(held, axis=1), "head", bit)
        if first is not None:
            other, first = lax.optimization_barrier((other, first))
            first = None
        high = (me // bit) % 2 == 1
        merged = []
        for i, own in enumerate(held):
            theirs = other[:, i * columns : (i + 1) * columns]
            merged += [jnp.where(high, theirs, own), jnp.where(high, own, theirs)]
        held = merged
        bit //= 2
    return held


def scatter_heads(partial):
    me = lax.axis_index("head")
    size = lax.axis_size("head")
    share = partial.shape[1] // size
    held = [partial[:, i * share : (i + 1) * share] for i in range(size)]
    bit = 1
    while bit < size:
        high = (me // bit) % 2 == 1
        couples = list(zip(held[0::2], held[1::2]))
        given = jnp.concatenate([jnp.where(high, a, b).astype(BF) for a, b in couples], axis=1)
        other = swap(given, "head", bit)
        held = [
            jnp.where(high, b, a) + other[:, i * share : (i + 1) * share].astype(F32)
            for i, (a, b) in enumerate(couples)
        ]
        bit *= 2
    return held[0].astype(BF)


def with_doc(state, doc):
    rows = jnp.broadcast_to(doc.astype(BF)[:, None], (16, state.shape[-1]))
    return jnp.concatenate([state.astype(BF).reshape(-1, state.shape[-1]), rows], axis=0)


def window(total, sign, first=None):
    rows = lax.broadcasted_iota(jnp.int32, (total.shape[0], 1), 0) < total.shape[0] - 16
    span = 1
    while span < lax.axis_size("seq") // 2:
        far = shift(total, sign * span)
        if first is not None and 4 * span >= lax.axis_size("seq"):
            far, first = lax.optimization_barrier((far, first))
        same = (far[-16:-15] == total[-16:-15]) & rows
        total = total + jnp.where(same, far, jnp.zeros_like(far))
        span *= 2
    return total


def plain(queries, key_vectors, value_vectors, doc_ids, out_weight, grad_out):
    n = lax.axis_size("seq")
    m = lax.axis_size("head")
    length, heads, dh = queries.shape
    place = lax.axis_index("seq")
    parity = place % 2
    line = n // 2
    where_on_line = place // 2
    columns = out_weight.shape[1]
    width = columns // n

    docs = doc_ids.astype(F32)
    tail = (docs == docs[-1]).astype(BF)
    own_state = jnp.einsum(
        "shd,she->hde", key_vectors * tail[:, None, None], value_vectors, preferred_element_type=F32
    )
    near_flat = shift(with_doc(own_state, docs[-1:]), 1)
    own_gathered = gather_heads(grad_out, near_flat)
    near_flat, grad_out = lax.optimization_barrier((near_flat, grad_out))
    flat = window(near_flat, 1)
    before = flat[-16, :1].astype(F32)
    state_low = flat[:-16].reshape(own_state.shape)

    causal = lax.broadcasted_iota(jnp.int32, (length, length), 0) >= lax.broadcasted_iota(
        jnp.int32, (length, length), 1
    )
    pairs = causal & (docs[:, None] == docs[None, :])
    reads = (docs == before[0]).astype(F32)
    scores = jnp.einsum("thd,shd->hts", queries, key_vectors, preferred_element_type=F32)
    scores_low = jnp.where(pairs[None], scores, 0.0).astype(BF)
    attn = jnp.einsum("hts,she->the", scores_low, value_vectors, preferred_element_type=F32)
    attn = attn + reads[:, None, None] * jnp.einsum(
        "thd,hde->the", queries, state_low, preferred_element_type=F32
    )
    scale = lax.rsqrt(jnp.mean(attn * attn, axis=-1, keepdims=True) + 1e-05)
    normed_f = attn * scale
    normed = normed_f.astype(BF).reshape(length, -1)
    partner_normed = swap(normed, "seq", 1)

    share = columns // m
    odd = parity == 1
    for_partner = [
        jnp.where(odd, grad_out[:, i : i + width], grad_out[:, i + width : i + 2 * width])
        for i in range(0, share, 2 * width)
    ]
    from_partner = swap(jnp.concatenate(for_partner, axis=1), "seq", 1)
    cotangent = jnp.concatenate(own_gathered, axis=1)
    partner_cot = jnp.concatenate(gather_heads(from_partner, normed), axis=1)

    grad_normed = lax.dot_general(
        cotangent, out_weight, (((1,), (1,)), ((), ())), preferred_element_type=F32
    ).reshape(attn.shape)
    grad_attn = (
        scale * (grad_normed - normed_f * jnp.mean(grad_normed * normed_f, axis=-1, keepdims=True))
    ).astype(BF)
    head_mask = (docs == docs[0]).astype(BF)
    own_back = jnp.einsum(
        "thd,the->hde", queries * head_mask[:, None, None], grad_attn, preferred_element_type=F32
    )
    near_flat = shift(with_doc(own_back, docs[:1]), -1)

    def share_of(step):
        goal = (where_on_line + step) % line
        mine = lax.dynamic_slice_in_dim(cotangent, (2 * goal + parity) * width, width, 1)
        theirs = lax.dynamic_slice_in_dim(partner_cot, goal * width, width, 1)
        over_tokens = (((0,), (0,)), ((), ()))
        return lax.dot_general(
            normed, mine, over_tokens, preferred_element_type=F32
        ) + lax.dot_general(partner_normed, theirs, over_tokens, preferred_element_type=F32)

    terms = [share_of(step).astype(BF) for step in range(1, line)]
    terms, near_flat = lax.optimization_barrier((terms, near_flat))
    terms, grad_attn_in, normed_out = lax.optimization_barrier((terms, grad_attn, normed))
    partial_out = jnp.dot(normed_out, out_weight, preferred_element_type=F32)
    layer_out = scatter_heads(partial_out)
    flat = window(near_flat, -1, layer_out)
    after = flat[-16, :1].astype(F32)
    back_low = flat[:-16].reshape(own_back.shape)
    writes = (docs == after[0]).astype(F32)
    arrived = []
    for step, term in enumerate(terms, 1):
        route = [
            (2 * a + b, 2 * ((a + step) % line) + b) for a in range(line) for b in range(2)
        ]
        arrived.append(lax.ppermute(term, "seq", route))
    own_term = share_of(0)

    grad_scores = jnp.einsum("the,she->hts", grad_attn_in, value_vectors, preferred_element_type=F32)
    grad_scores = jnp.where(pairs[None], grad_scores, 0.0).astype(BF)
    grad_queries = jnp.einsum("hts,shd->thd", grad_scores, key_vectors, preferred_element_type=F32)
    grad_queries = grad_queries + reads[:, None, None] * jnp.einsum(
        "the,hde->thd", grad_attn_in, state_low, preferred_element_type=F32
    )
    grad_keys = jnp.einsum("hts,thd->shd", grad_scores, queries, preferred_element_type=F32)
    grad_keys = grad_keys + writes[:, None, None] * jnp.einsum(
        "she,hde->shd", value_vectors, back_low, preferred_element_type=F32
    )
    grad_values = jnp.einsum("hts,the->she", scores_low, grad_attn_in, preferred_element_type=F32)
    grad_values = grad_values + writes[:, None, None] * jnp.einsum(
        "shd,hde->she", key_vectors, back_low, preferred_element_type=F32
    )
    arrived, layer_out = lax.optimization_barrier((arrived, layer_out))
    grad_weight = own_term
    for part in arrived:
        grad_weight = grad_weight + part.astype(F32)
    return (
        layer_out,
        grad_queries.astype(BF),
        grad_keys.astype(BF),
        grad_values.astype(BF),
        grad_weight,
    )


def fits(mesh, columns, heads, dh):
    n, m = mesh.shape["seq"], mesh.shape["head"]
    return m == 4 and n == 2 * m and columns % (128 * n) == 0 and heads == 8 and dh == 128


def choose(mesh):
    def shards(queries, key_vectors, value_vectors, doc_ids, out_weight, grad_out):
        heads, dh = queries.shape[1:]
        form = fused if fits(mesh, out_weight.shape[1], heads, dh) else plain
        return form(queries, key_vectors, value_vectors, doc_ids, out_weight, grad_out)

    return shards


def solution(mesh):
    placed = (
        P("seq", "head", None),
        P("seq", "head", None),
        P("seq", "head", None),
        P("seq"),
        P("head", None),
        P("seq", "head"),
    )
    return jax.shard_map(
        choose(mesh),
        mesh=mesh,
        in_specs=placed,
        out_specs=(
            P("seq", "head"),
            P("seq", "head", None),
            P("seq", "head", None),
            P("seq", "head", None),
            P("head", "seq"),
        ),
        check_vma=False,
    )
```

```python
import functools

import jax
import jax.numpy as jnp
from jax import lax
from jax.experimental import pallas as pl
from jax.experimental.pallas import tpu as pltpu
from jax.sharding import PartitionSpec as P


BF = jnp.bfloat16
F32 = jnp.float32
MESH = pl.DeviceIdType.MESH


def dot_nn(a, b):
    return lax.dot_general(a, b, (((1,), (0,)), ((), ())), preferred_element_type=F32)


def dot_nt(a, b):
    return lax.dot_general(a, b, (((1,), (1,)), ((), ())), preferred_element_type=F32)


def dot_tn(a, b):
    return lax.dot_general(a, b, (((0,), (0,)), ((), ())), preferred_element_type=F32)


def loop(count, body):
    lax.fori_loop(0, count, lambda i, _: (body(i), None)[1], None)


def kernel(
    sizes,
    docs_ref, q_hbm, k_hbm, v_hbm, w_hbm, go_hbm,
    lo_out, gq_out, gk_out, gv_out, gw_out,
    raw_q, raw_k, raw_v, q, k, v, w, g, p, mask, scores, attn, gn, normed, nt, ntp, ga,
    f_own, f_mate, f_next, f_carry, f_low,
    r_own, r_mate, r_next, r_carry, r_low,
    lc_send, lc_recv, lx_send, lx_recv, lo_acc, lo_fin,
    sb, ub, db, gacc, part,
    doc_col, reads, writes, tail, front,
    in_sem, g_send, g_recv, p_send, p_recv, f_send, f_recv, r_send, r_recv,
    n_send, n_recv, lc_ss, lc_rs, lx_ss, lx_rs, u_ss, u_rs, d_ss, d_rs, out_sem,
):
    n, m, heads, length, dh, share, width = sizes
    line = n // 2
    pairs = heads // 2
    rows = 2 * dh
    tile = 2 * dh
    s = lax.axis_index("seq")
    h = lax.axis_index("head")
    a = s // 2
    b = s % 2
    hc = h % 2
    hx = h // 2
    core = h + 1 - 2 * hc
    across = h + 2 - 4 * hx
    both = core + 2 - 4 * hx
    mate = s + 1 - 2 * b
    at_end = (a == 0) | (a == line - 1)

    barrier = pltpu.get_barrier_semaphore()

    def greet(seq, head):
        pl.semaphore_signal(barrier, inc=1, device_id=(seq, head), device_id_type=MESH)

    def local(src, dst, i):
        return pltpu.make_async_copy(src, dst, in_sem.at[i])

    def remote(src, dst, ss, rs, seq, head):
        return pltpu.make_async_remote_copy(
            src_ref=src, dst_ref=dst, send_sem=ss, recv_sem=rs,
            device_id=(seq, head), device_id_type=MESH,
        )

    loads = [
        local(go_hbm, g.at[h], 0), local(k_hbm, raw_k, 1), local(v_hbm, raw_v, 2),
        local(q_hbm, raw_q, 3), local(w_hbm, w, 4),
    ]
    for copy in loads:
        copy.start()
    greet(s, core)
    greet(s, across)
    greet(mate, h)

    @pl.when(a < line - 1)
    def _():
        greet(s + 2, h)

    @pl.when(a > 0)
    def _():
        greet(s - 2, h)

    def spot(cond):
        return jnp.where(cond, 1, 0)

    docs_row = docs_ref[...].astype(F32)
    doc_col[...] = jnp.broadcast_to(docs_row, (dh, length)).T
    last_doc = doc_col[pl.ds(length - 1, 1), :]
    first_doc = doc_col[pl.ds(0, 1), :]
    tail[...] = jnp.where(doc_col[...] == last_doc, 1.0, 0.0).astype(BF)
    front[...] = jnp.where(doc_col[...] == first_doc, 1.0, 0.0).astype(BF)
    for c in range(pairs):
        f_own[c, pl.ds(rows, 16), :] = jnp.broadcast_to(last_doc, (16, dh)).astype(BF)
        r_own[c, pl.ds(rows, 16), :] = jnp.broadcast_to(first_doc, (16, dh)).astype(BF)

    def blank(ref):
        ref[...] = jnp.zeros_like(ref)
        for c in range(pairs):
            ref[c, pl.ds(rows, 16), :] = jnp.full((16, dh), -1.0, BF)

    @pl.when(a == 0)
    def _():
        blank(f_carry)

    @pl.when(a == line - 1)
    def _():
        blank(r_carry)

    pl.semaphore_wait(barrier, 3 + spot(a < line - 1) + spot(a > 0))

    loads[0].wait()
    theirs = pl.ds(pl.multiple_of((1 - b) * width, 128), width)
    ours = pl.ds(pl.multiple_of(b * width, 128), width)

    def g_part(slot, at, i, to):
        part_of = g.at[slot, at[0], at[1]]
        return remote(part_of, part_of, g_send.at[i], g_recv.at[i], s, to)

    whole = pl.ds(0, length)
    head_rows = 3 * length // 8
    slices = pl.ds(0, head_rows), pl.ds(head_rows, length - head_rows)
    g_core = g_part(h, (whole, pl.ds(0, share)), 0, core)
    g_ours = g_part(h, (whole, ours), 1, across)
    g_theirs = g_part(h, (whole, theirs), 2, across)
    g_pass_ours = g_part(across, (whole, ours), 3, core)
    g_pass_theirs = g_part(across, (whole, theirs), 4, core)
    p_mates = [
        remote(g.at[h, at, theirs], p.at[h, at, :], p_send.at[i], p_recv.at[i], mate, h)
        for i, at in enumerate(slices)
    ]
    p_acrosses = [
        remote(p.at[h, at, :], p.at[h, at, :], p_send.at[4 + i], p_recv.at[4 + i], s, across)
        for i, at in enumerate(slices)
    ]
    p_core = remote(p.at[h], p.at[h], p_send.at[2], p_recv.at[2], s, core)
    p_pass = remote(p.at[across], p.at[across], p_send.at[3], p_recv.at[3], s, core)
    g_ours.start()
    p_mates[0].start()
    g_core.start()

    class States:
        def __init__(self, split, sign, step, odd, own, mate_ref, after, carry, low, ss, rs):
            self.split, self.sign, self.step, self.odd = split, sign, step, odd
            self.own, self.mate, self.after, self.carry, self.low = own, mate_ref, after, carry, low
            self.ss, self.rs = ss, rs

        def swap(self, c):
            return remote(
                self.own.at[c], self.mate.at[c], self.ss.at[0, c], self.rs.at[0, c], mate, h
            )

        def onward(self, c):
            return remote(
                self.after.at[c], self.carry.at[c], self.ss.at[1, c], self.rs.at[1, c],
                s + self.sign * 2, h,
            )

        def values(self, ref, c):
            return (
                ref[c, pl.ds(0, rows), :].astype(F32),
                ref[c, pl.ds(rows, 1), :].astype(F32),
            )

        def add(self, base, more):
            same = jnp.broadcast_to(jnp.where(base[1] == more[1], 1.0, 0.0), (rows, dh))
            return base[0] + more[0] * same, base[1]

        def members(self, c):
            mine, other = self.values(self.own, c), self.values(self.mate, c)
            odd = self.odd == 1
            early = tuple(jnp.where(odd, y, x) for x, y in zip(mine, other))
            late = tuple(jnp.where(odd, x, y) for x, y in zip(mine, other))
            return early, late

        def forward(self, c):
            early, late = self.members(c)
            total, doc = self.add(self.add(late, early), self.values(self.carry, c))
            self.after[c, pl.ds(0, rows), :] = total.astype(BF)
            self.after[c, pl.ds(rows, 16), :] = jnp.broadcast_to(doc, (16, dh)).astype(BF)
            self.onward(c).start()

        def settle(self, c):
            early, _ = self.members(c)
            carry = self.values(self.carry, c)
            odd = self.odd == 1
            total = jnp.where(odd, self.add(early, carry)[0], carry[0]).astype(BF)
            self.low[2 * c] = total[:dh]
            self.low[2 * c + 1] = total[dh:]

        def open(self, c):
            self.swap(c).wait_recv()

            @pl.when((self.step == 0) & self.mine(c))
            def _():
                self.forward(c)

        def mine(self, c):
            return (c % 2 == b) if self.split else (c >= 0)

        def share(self, c):
            return remote(
                self.carry.at[c], self.carry.at[c], self.ss.at[2, c], self.rs.at[2, c], mate, h
            )

        def relay(self, c):
            @pl.when((self.step > 0) & self.mine(c))
            def _():
                self.onward(c).wait_recv()
                self.share(c).start()

                @pl.when(self.step < line - 1)
                def _():
                    self.forward(c)

        def shared(self, c):
            @pl.when((self.step > 0) & ~self.mine(c))
            def _():
                self.share(c).wait_recv()

        def serve(self, c):
            @pl.when((self.step > 0) & (c > 0))
            def _():
                self.onward(c).wait_recv()

            @pl.when((self.step > 0) & (self.step < line - 1))
            def _():
                self.forward(c)

            self.settle(c)

        def reached(self):
            early, _ = self.members(0)
            doc = jnp.where(self.odd == 1, early[1], self.values(self.carry, 0)[1])
            return jnp.where(doc_col[...] == doc, 1.0, 0.0)

        def drain(self, c):
            self.swap(c).wait_send()

            @pl.when((self.step < line - 1) & self.mine(c))
            def _():
                self.onward(c).wait_send()

            if self.split:
                @pl.when((self.step > 0) & self.mine(c))
                def _():
                    self.share(c).wait_send()

    ahead = States(False, 1, a, b, f_own, f_mate, f_next, f_carry, f_low, f_send, f_recv)
    behind = States(
        True, -1, line - 1 - a, 1 - b, r_own, r_mate, r_next, r_carry, r_low, r_send, r_recv
    )

    some = 64

    def by_head(raw, ref):
        def block(i):
            at = pl.ds(pl.multiple_of(i * some, some), some)
            ref[:, at, :] = jnp.swapaxes(raw[at], 0, 1)

        loop(length // some, block)

    def by_token(ref, raw):
        def block(i):
            at = pl.ds(pl.multiple_of(i * some, some), some)
            raw[at] = jnp.swapaxes(ref[:, at, :], 0, 1)

        loop(length // some, block)

    loads[1].wait()
    by_head(raw_k, k)
    loads[2].wait()
    by_head(raw_v, v)

    def own_state(c):
        for i in range(2):
            f_own[c, pl.ds(i * dh, dh), :] = dot_tn(
                k[2 * c + i] * tail[...], v[2 * c + i]
            ).astype(BF)
        ahead.swap(c).start()

    own_state(0)
    p_mates[1].start()
    loop(pairs - 1, lambda c: own_state(c + 1))
    p_mates[0].wait_recv()
    p_acrosses[0].start()
    loads[3].wait()
    by_head(raw_q, q)

    for i in range(length // dh):
        at = pl.ds(i * dh, dh)
        col = doc_col[at, :][:, :1]
        t_pos = lax.broadcasted_iota(jnp.int32, (dh, length), 0) + i * dh
        s_pos = lax.broadcasted_iota(jnp.int32, (dh, length), 1)
        ok = (t_pos >= s_pos) & (col == docs_row)
        mask[at, :] = jnp.where(ok, 1.0, 0.0).astype(BF)

    ahead.open(0)

    def local_attention(head):
        scores[head] = dot_nt(q[head], k[head]).astype(BF) * mask[...]
        attn[head] = dot_nn(scores[head], v[head])

    def between(low, high, body):
        lax.fori_loop(low, high, lambda i, _: (body(i), None)[1], None)

    def cotangents(pair, slot):
        return dot_nt(
            g[slot],
            w[pl.ds(pl.multiple_of(pair * tile, tile), tile), pl.ds(pl.multiple_of(slot * share, 128), share)],
        )

    def first_cotangents(pair):
        gn[pair] = cotangents(pair, h) + cotangents(pair, core)

    def hand_on():
        p_mates[1].wait_recv()
        p_acrosses[1].start()
        p_core.start()
        g_theirs.start()
        g_ours.wait_recv()
        g_pass_ours.start()
        loads[4].wait()
        g_core.wait_recv()

        @pl.when(a == line - 1)
        def _():
            loop(pairs, first_cotangents)

    def nt_copy(head):
        at = pl.ds(pl.multiple_of(head * dh, dh), dh)
        return remote(nt.at[at, :], ntp.at[at, :], n_send.at[head], n_recv.at[head], mate, h)

    def scale_of(value):
        return lax.rsqrt(jnp.mean(value * value, axis=-1, keepdims=True) + 1e-05)

    soon = jnp.where(at_end, 1, pairs // 2)

    def normalise(c):
        ahead.serve(c)
        for i in range(2):
            head = 2 * c + i
            value = attn[head] + reads[...] * dot_nn(q[head], f_low[head])
            attn[head] = value
            low = (value * scale_of(value)).astype(BF)
            at = pl.ds(pl.multiple_of(head * dh, dh), dh)
            normed[:, at] = low
            nt[at, :] = low.T

            @pl.when(c < soon)
            def _():
                nt_copy(head).start()

    late = a >= line // 2
    enough = jnp.where(late, heads, heads // 2)
    between(0, enough, local_attention)

    @pl.when(late)
    def _():
        hand_on()

    @pl.when(a > 0)
    def _():
        ahead.onward(0).wait_recv()

    reads[...] = ahead.reached()
    normalise(0)
    between(enough, heads, local_attention)

    @pl.when(~late)
    def _():
        hand_on()

    loop(pairs - 1, lambda c: ahead.open(c + 1))
    between(1, jnp.where(at_end, 1, pairs), normalise)

    @pl.when(a < line - 1)
    def _():
        loop(pairs, first_cotangents)

    for copy in p_acrosses:
        copy.wait_recv()
    p_pass.start()
    p_core.wait_recv()
    g_pass_ours.wait_recv()
    p_pass.wait_recv()

    def rest_of_cotangents():
        g_theirs.wait_recv()
        g_pass_theirs.start()
        g_pass_theirs.wait_recv()

    def grad_attention(c):
        pair_gn = gn[c] + cotangents(c, across) + cotangents(c, both)
        for i in range(2):
            head = 2 * c + i
            value = attn[head]
            scale = scale_of(value)
            norm = value * scale
            grad = pair_gn[:, i * dh : (i + 1) * dh]
            low = (scale * (grad - norm * jnp.mean(grad * norm, axis=-1, keepdims=True))).astype(BF)
            ga[head] = low
            r_own[c, pl.ds(i * dh, dh), :] = dot_tn(q[head] * front[...], low).astype(BF)
        behind.swap(c).start()

    def gradients():
        rest_of_cotangents()
        loop(pairs, grad_attention)
        between(2 * soon, heads, lambda head: nt_copy(head).start())

    def u_copy(d, j):
        at = pl.ds(pl.multiple_of(j * rows, rows), rows)
        return remote(sb.at[d, at, :], ub.at[d, at, :], u_ss.at[d, j], u_rs.at[d, j], s + 2, h)

    def d_copy(d, j):
        at = pl.ds(pl.multiple_of(j * rows, rows), rows)
        return remote(sb.at[d, at, :], db.at[d, at, :], d_ss.at[d, j], d_rs.at[d, j], s - 2, h)

    def weight_terms(first, count):
        for j in range(first, first + count):
            nt_copy(2 * j).wait_recv()
            nt_copy(2 * j + 1).wait_recv()

        def one(i):
            r = i // count
            j = first + i % count
            at = pl.ds(pl.multiple_of(j * rows, rows), rows)
            d = jnp.where(r % 2 == 0, line - 1 - r // 2, r // 2)
            d = jnp.where(a < line // 2, d, line - 1 - d)
            part[...] = dot_nn(nt[at, :], g[d, :, ours]) + dot_nn(ntp[at, :], p[d])

            @pl.when((d > a) & (a > 0))
            def _():
                u_copy(d, j).wait_recv()
                part[...] += ub[d, at, :].astype(F32)

            @pl.when((d < a) & (a < line - 1))
            def _():
                d_copy(d, j).wait_recv()
                part[...] += db[d, at, :].astype(F32)

            @pl.when(d == a)
            def _():
                gacc[at, :] = part[...]

            @pl.when(d != a)
            def _():
                sb[d, at, :] = part[...].astype(BF)

            @pl.when(d > a)
            def _():
                u_copy(d, j).start()

            @pl.when(d < a)
            def _():
                d_copy(d, j).start()

        loop(line * count, one)

    @pl.when(~at_end)
    def _():
        gradients()

    weight_terms(0, 1)

    @pl.when(at_end)
    def _():
        between(1, pairs, normalise)
        gradients()

    loop(pairs, behind.open)

    @pl.when(at_end)
    def _():
        weight_terms(1, 1)

    tiles = share // tile

    def projected(d, t):
        at = pl.ds(pl.multiple_of(d * share + t * tile, 128), tile)
        return dot_nn(normed[...], w[:, at])

    def lc_copy(side):
        return remote(
            lc_send.at[side], lc_recv.at[side], lc_ss.at[side], lc_rs.at[side], s, core
        )

    lx_copy = remote(lx_send, lx_recv, lx_ss.at[0], lx_rs.at[0], s, across)

    def columns(t):
        return pl.ds(pl.multiple_of(t * tile, tile), tile)

    for side in (1 - hx, hx):
        def give(t, side=side):
            lc_send[side, :, columns(t)] = projected(2 * side + 1 - hc, t).astype(BF)

        loop(tiles, give)
        lc_copy(side).start()

    lc_copy(1 - hx).wait_recv()

    def cross(t):
        lx_send[:, columns(t)] = (
            projected(2 * (1 - hx) + hc, t) + lc_recv[1 - hx, :, columns(t)].astype(F32)
        ).astype(BF)

    loop(tiles, cross)
    lx_copy.start()

    def serve_back():
        loop(pairs, behind.relay)
        loop(pairs, behind.shared)
        writes[...] = behind.reached()
        loop(pairs, behind.settle)

    @pl.when(~at_end)
    def _():
        serve_back()
        weight_terms(1, 1)

    @pl.when(at_end)
    def _():
        weight_terms(2, pairs - 2)

    def backward(c):
        for i in range(2):
            head = 2 * c + i
            grad = ga[head]
            gs = dot_nt(grad, v[head]).astype(BF) * mask[...]
            gq = dot_nn(gs, k[head]) + reads[...] * dot_nt(grad, f_low[head])
            attn[head] = dot_tn(gs, q[head])
            gn[c, :, pl.ds(i * dh, dh)] = dot_tn(scores[head], grad)
            q[head] = gq.astype(BF)

    loop(pairs, backward)

    lc_copy(hx).wait_recv()

    def keep(t):
        lo_acc[:, columns(t)] = projected(h, t) + lc_recv[hx, :, columns(t)].astype(F32)

    loop(tiles, keep)

    def out_copy(src, dst, i):
        return pltpu.make_async_copy(src, dst, out_sem.at[i])

    outs = []

    def give_back(ref, raw, out, i):
        by_token(ref, raw)
        outs.append(out_copy(raw, out, i))
        outs[-1].start()

    give_back(q, raw_q, gq_out, 0)

    @pl.when(at_end)
    def _():
        serve_back()

    def backward_states(c):
        for i in range(2):
            head = 2 * c + i
            gk = attn[head] + writes[...] * dot_nt(v[head], r_low[head])
            gv = gn[c, :, pl.ds(i * dh, dh)] + writes[...] * dot_nn(k[head], r_low[head])
            k[head] = gk.astype(BF)
            v[head] = gv.astype(BF)

    loop(pairs, backward_states)
    give_back(k, raw_k, gk_out, 1)
    give_back(v, raw_v, gv_out, 2)

    @pl.when(~at_end)
    def _():
        weight_terms(2, pairs - 2)

    lx_copy.wait_recv()
    lo_fin[...] = (lo_acc[...] + lx_recv[...].astype(F32)).astype(BF)
    outs.append(out_copy(lo_fin, lo_out, 3))
    outs[-1].start()

    def finish(j):
        at = pl.ds(pl.multiple_of(j * rows, rows), rows)

        @pl.when(a > 0)
        def _():
            u_copy(a, j).wait_recv()
            gacc[at, :] += ub[a, at, :].astype(F32)

        @pl.when(a < line - 1)
        def _():
            d_copy(a, j).wait_recv()
            gacc[at, :] += db[a, at, :].astype(F32)

    loop(pairs, finish)
    outs.append(out_copy(gacc, gw_out, 4))
    outs[-1].start()

    for copy in (
        g_core, g_ours, g_theirs, g_pass_ours, g_pass_theirs,
        *p_mates, *p_acrosses, p_core, p_pass, lx_copy,
    ):
        copy.wait_send()
    for side in range(2):
        lc_copy(side).wait_send()

    def drain(c):
        nt_copy(2 * c).wait_send()
        nt_copy(2 * c + 1).wait_send()
        ahead.drain(c)
        behind.drain(c)

        def lines(d):
            @pl.when(d > a)
            def _():
                u_copy(d, c).wait_send()

            @pl.when(d < a)
            def _():
                d_copy(d, c).wait_send()

        loop(line, lines)

    loop(pairs, drain)
    for copy in outs:
        copy.wait()


def fused(queries, key_vectors, value_vectors, doc_ids, out_weight, grad_out):
    n = lax.axis_size("seq")
    m = lax.axis_size("head")
    length, heads, dh = queries.shape
    feats, columns = out_weight.shape
    share = columns // m
    width = columns // n
    line = n // 2
    pairs = heads // 2
    docs = doc_ids.reshape(1, length)
    vm = pltpu.VMEM
    heads_bf = vm((heads, length, dh), BF)
    state = vm((pairs, 2 * dh + 16, dh), BF)
    low = vm((heads, dh, dh), BF)
    terms = vm((line, feats, width), BF)
    dma = pltpu.SemaphoreType.DMA
    by_token = vm((length, heads, dh), BF)
    scratch = [
        by_token, by_token, by_token,
        heads_bf, heads_bf, heads_bf,
        vm((feats, columns), BF),
        vm((m, length, share), BF),
        vm((m, length, width), BF),
        vm((length, length), BF),
        vm((heads, length, length), BF),
        vm((heads, length, dh), F32),
        vm((pairs, length, 2 * dh), F32),
        vm((length, feats), BF),
        vm((feats, length), BF),
        vm((feats, length), BF),
        heads_bf,
        state, state, state, state, low,
        state, state, state, state, low,
        vm((2, length, share), BF), vm((2, length, share), BF),
        vm((length, share), BF), vm((length, share), BF),
        vm((length, share), F32), vm((length, share), BF),
        terms, terms, terms,
        vm((feats, width), F32), vm((2 * dh, width), F32),
        vm((length, dh), F32), vm((length, dh), F32), vm((length, dh), F32),
        vm((length, dh), BF), vm((length, dh), BF),
        dma((5,)), dma((5,)), dma((5,)), dma((6,)), dma((6,)),
        dma((2, pairs)), dma((2, pairs)), dma((3, pairs)), dma((3, pairs)),
        dma((heads,)), dma((heads,)), dma((2,)), dma((2,)), dma((1,)), dma((1,)),
        dma((line, pairs)), dma((line, pairs)), dma((line, pairs)), dma((line, pairs)),
        dma((5,)),
    ]
    anywhere = pl.BlockSpec(memory_space=pl.ANY)
    grads = jax.ShapeDtypeStruct((length, heads, dh), BF)
    lo, gq, gk, gv, gw = pl.pallas_call(
        functools.partial(kernel, (n, m, heads, length, dh, share, width)),
        out_shape=(
            jax.ShapeDtypeStruct((length, share), BF), grads, grads, grads,
            jax.ShapeDtypeStruct((feats, width), F32),
        ),
        in_specs=[pl.BlockSpec(memory_space=pltpu.VMEM)] + [anywhere] * 5,
        out_specs=(anywhere,) * 5,
        scratch_shapes=scratch,
        compiler_params=pltpu.CompilerParams(
            collective_id=0, has_side_effects=True, vmem_limit_bytes=60 << 20
        ),
    )(docs, queries, key_vectors, value_vectors, out_weight, grad_out)
    return lo, gq, gk, gv, gw


def shift(block, distance):
    n = lax.axis_size("seq")
    route = [(i, i + distance) for i in range(n) if 0 <= i + distance < n]
    return lax.ppermute(block, "seq", route)


def swap(block, axis, bit):
    n = lax.axis_size(axis)
    return lax.ppermute(block, axis, [(i, i ^ bit) for i in range(n)])


def gather_heads(block, first):
    me = lax.axis_index("head")
    bit = lax.axis_size("head") // 2
    columns = block.shape[1]
    held = [block]
    while bit:
        other = swap(jnp.concatenate(held, axis=1), "head", bit)
        if first is not None:
            other, first = lax.optimization_barrier((other, first))
            first = None
        high = (me // bit) % 2 == 1
        merged = []
        for i, own in enumerate(held):
            theirs = other[:, i * columns : (i + 1) * columns]
            merged += [jnp.where(high, theirs, own), jnp.where(high, own, theirs)]
        held = merged
        bit //= 2
    return held


def scatter_heads(partial):
    me = lax.axis_index("head")
    size = lax.axis_size("head")
    share = partial.shape[1] // size
    held = [partial[:, i * share : (i + 1) * share] for i in range(size)]
    bit = 1
    while bit < size:
        high = (me // bit) % 2 == 1
        couples = list(zip(held[0::2], held[1::2]))
        given = jnp.concatenate([jnp.where(high, a, b).astype(BF) for a, b in couples], axis=1)
        other = swap(given, "head", bit)
        held = [
            jnp.where(high, b, a) + other[:, i * share : (i + 1) * share].astype(F32)
            for i, (a, b) in enumerate(couples)
        ]
        bit *= 2
    return held[0].astype(BF)


def with_doc(state, doc):
    rows = jnp.broadcast_to(doc.astype(BF)[:, None], (16, state.shape[-1]))
    return jnp.concatenate([state.astype(BF).reshape(-1, state.shape[-1]), rows], axis=0)


def window(total, sign, first=None):
    rows = lax.broadcasted_iota(jnp.int32, (total.shape[0], 1), 0) < total.shape[0] - 16
    span = 1
    while span < lax.axis_size("seq") // 2:
        far = shift(total, sign * span)
        if first is not None and 4 * span >= lax.axis_size("seq"):
            far, first = lax.optimization_barrier((far, first))
        same = (far[-16:-15] == total[-16:-15]) & rows
        total = total + jnp.where(same, far, jnp.zeros_like(far))
        span *= 2
    return total


def plain(queries, key_vectors, value_vectors, doc_ids, out_weight, grad_out):
    n = lax.axis_size("seq")
    m = lax.axis_size("head")
    length, heads, dh = queries.shape
    place = lax.axis_index("seq")
    parity = place % 2
    line = n // 2
    where_on_line = place // 2
    columns = out_weight.shape[1]
    width = columns // n

    docs = doc_ids.astype(F32)
    tail = (docs == docs[-1]).astype(BF)
    own_state = jnp.einsum(
        "shd,she->hde", key_vectors * tail[:, None, None], value_vectors, preferred_element_type=F32
    )
    near_flat = shift(with_doc(own_state, docs[-1:]), 1)
    own_gathered = gather_heads(grad_out, near_flat)
    near_flat, grad_out = lax.optimization_barrier((near_flat, grad_out))
    flat = window(near_flat, 1)
    before = flat[-16, :1].astype(F32)
    state_low = flat[:-16].reshape(own_state.shape)

    causal = lax.broadcasted_iota(jnp.int32, (length, length), 0) >= lax.broadcasted_iota(
        jnp.int32, (length, length), 1
    )
    pairs = causal & (docs[:, None] == docs[None, :])
    reads = (docs == before[0]).astype(F32)
    scores = jnp.einsum("thd,shd->hts", queries, key_vectors, preferred_element_type=F32)
    scores_low = jnp.where(pairs[None], scores, 0.0).astype(BF)
    attn = jnp.einsum("hts,she->the", scores_low, value_vectors, preferred_element_type=F32)
    attn = attn + reads[:, None, None] * jnp.einsum(
        "thd,hde->the", queries, state_low, preferred_element_type=F32
    )
    scale = lax.rsqrt(jnp.mean(attn * attn, axis=-1, keepdims=True) + 1e-05)
    normed_f = attn * scale
    normed = normed_f.astype(BF).reshape(length, -1)
    partner_normed = swap(normed, "seq", 1)

    share = columns // m
    odd = parity == 1
    for_partner = [
        jnp.where(odd, grad_out[:, i : i + width], grad_out[:, i + width : i + 2 * width])
        for i in range(0, share, 2 * width)
    ]
    from_partner = swap(jnp.concatenate(for_partner, axis=1), "seq", 1)
    cotangent = jnp.concatenate(own_gathered, axis=1)
    partner_cot = jnp.concatenate(gather_heads(from_partner, normed), axis=1)

    grad_normed = lax.dot_general(
        cotangent, out_weight, (((1,), (1,)), ((), ())), preferred_element_type=F32
    ).reshape(attn.shape)
    grad_attn = (
        scale * (grad_normed - normed_f * jnp.mean(grad_normed * normed_f, axis=-1, keepdims=True))
    ).astype(BF)
    head_mask = (docs == docs[0]).astype(BF)
    own_back = jnp.einsum(
        "thd,the->hde", queries * head_mask[:, None, None], grad_attn, preferred_element_type=F32
    )
    near_flat = shift(with_doc(own_back, docs[:1]), -1)

    def share_of(step):
        goal = (where_on_line + step) % line
        mine = lax.dynamic_slice_in_dim(cotangent, (2 * goal + parity) * width, width, 1)
        theirs = lax.dynamic_slice_in_dim(partner_cot, goal * width, width, 1)
        over_tokens = (((0,), (0,)), ((), ()))
        return lax.dot_general(
            normed, mine, over_tokens, preferred_element_type=F32
        ) + lax.dot_general(partner_normed, theirs, over_tokens, preferred_element_type=F32)

    terms = [share_of(step).astype(BF) for step in range(1, line)]
    terms, near_flat = lax.optimization_barrier((terms, near_flat))
    terms, grad_attn_in, normed_out = lax.optimization_barrier((terms, grad_attn, normed))
    partial_out = jnp.dot(normed_out, out_weight, preferred_element_type=F32)
    layer_out = scatter_heads(partial_out)
    flat = window(near_flat, -1, layer_out)
    after = flat[-16, :1].astype(F32)
    back_low = flat[:-16].reshape(own_back.shape)
    writes = (docs == after[0]).astype(F32)
    arrived = []
    for step, term in enumerate(terms, 1):
        route = [
            (2 * a + b, 2 * ((a + step) % line) + b) for a in range(line) for b in range(2)
        ]
        arrived.append(lax.ppermute(term, "seq", route))
    own_term = share_of(0)

    grad_scores = jnp.einsum("the,she->hts", grad_attn_in, value_vectors, preferred_element_type=F32)
    grad_scores = jnp.where(pairs[None], grad_scores, 0.0).astype(BF)
    grad_queries = jnp.einsum("hts,shd->thd", grad_scores, key_vectors, preferred_element_type=F32)
    grad_queries = grad_queries + reads[:, None, None] * jnp.einsum(
        "the,hde->thd", grad_attn_in, state_low, preferred_element_type=F32
    )
    grad_keys = jnp.einsum("hts,thd->shd", grad_scores, queries, preferred_element_type=F32)
    grad_keys = grad_keys + writes[:, None, None] * jnp.einsum(
        "she,hde->shd", value_vectors, back_low, preferred_element_type=F32
    )
    grad_values = jnp.einsum("hts,the->she", scores_low, grad_attn_in, preferred_element_type=F32)
    grad_values = grad_values + writes[:, None, None] * jnp.einsum(
        "shd,hde->she", key_vectors, back_low, preferred_element_type=F32
    )
    arrived, layer_out = lax.optimization_barrier((arrived, layer_out))
    grad_weight = own_term
    for part in arrived:
        grad_weight = grad_weight + part.astype(F32)
    return (
        layer_out,
        grad_queries.astype(BF),
        grad_keys.astype(BF),
        grad_values.astype(BF),
        grad_weight,
    )


def fits(mesh, columns, heads, dh):
    n, m = mesh.shape["seq"], mesh.shape["head"]
    return m == 4 and n == 2 * m and columns % (128 * n) == 0 and heads == 8 and dh == 128


def choose(mesh):
    def shards(queries, key_vectors, value_vectors, doc_ids, out_weight, grad_out):
        heads, dh = queries.shape[1:]
        form = fused if fits(mesh, out_weight.shape[1], heads, dh) else plain
        return form(queries, key_vectors, value_vectors, doc_ids, out_weight, grad_out)

    return shards


def solution(mesh):
    placed = (
        P("seq", "head", None),
        P("seq", "head", None),
        P("seq", "head", None),
        P("seq"),
        P("head", None),
        P("seq", "head"),
    )
    return jax.shard_map(
        choose(mesh),
        mesh=mesh,
        in_specs=placed,
        out_specs=(
            P("seq", "head"),
            P("seq", "head", None),
            P("seq", "head", None),
            P("seq", "head", None),
            P("head", "seq"),
        ),
        check_vma=False,
    )
```

```python
import functools

import jax
import jax.numpy as jnp
from jax import lax
from jax.experimental import pallas as pl
from jax.experimental.pallas import tpu as pltpu
from jax.sharding import PartitionSpec as P


BF = jnp.bfloat16
F32 = jnp.float32
MESH = pl.DeviceIdType.MESH


def dot_nn(a, b):
    return lax.dot_general(a, b, (((1,), (0,)), ((), ())), preferred_element_type=F32)


def dot_nt(a, b):
    return lax.dot_general(a, b, (((1,), (1,)), ((), ())), preferred_element_type=F32)


def dot_tn(a, b):
    return lax.dot_general(a, b, (((0,), (0,)), ((), ())), preferred_element_type=F32)


def loop(count, body):
    lax.fori_loop(0, count, lambda i, _: (body(i), None)[1], None)


def kernel(
    sizes,
    docs_ref, q_hbm, k_hbm, v_hbm, w_hbm, go_hbm,
    lo_fin, raw_q, raw_k, raw_v, gacc,
    q, k, v, w, g, p, mask, scores, attn, gn, normed, nt, ntp, ga,
    f_own, f_mate, f_next, f_carry, f_low,
    r_own, r_mate, r_next, r_carry, r_low,
    lc_send, lc_recv, lx_send, lx_recv, lo_acc,
    sb, ub, db, part,
    doc_col, reads, writes, tail, front,
    in_sem, g_send, g_recv, p_send, p_recv, f_send, f_recv, r_send, r_recv,
    n_send, n_recv, lc_ss, lc_rs, lx_ss, lx_rs, u_ss, u_rs, d_ss, d_rs,
):
    n, m, heads, length, dh, share, width = sizes
    line = n // 2
    pairs = heads // 2
    rows = 2 * dh
    tile = 2 * dh
    s = lax.axis_index("seq")
    h = lax.axis_index("head")
    a = s // 2
    b = s % 2
    hc = h % 2
    hx = h // 2
    core = h + 1 - 2 * hc
    across = h + 2 - 4 * hx
    both = core + 2 - 4 * hx
    mate = s + 1 - 2 * b
    at_end = (a == 0) | (a == line - 1)

    barrier = pltpu.get_barrier_semaphore()

    def greet(seq, head):
        pl.semaphore_signal(barrier, inc=1, device_id=(seq, head), device_id_type=MESH)

    def local(src, dst, i):
        return pltpu.make_async_copy(src, dst, in_sem.at[i])

    def remote(src, dst, ss, rs, seq, head):
        return pltpu.make_async_remote_copy(
            src_ref=src, dst_ref=dst, send_sem=ss, recv_sem=rs,
            device_id=(seq, head), device_id_type=MESH,
        )

    loads = [
        local(go_hbm, g.at[h], 0), local(k_hbm, raw_k, 1), local(v_hbm, raw_v, 2),
        local(q_hbm, raw_q, 3), local(w_hbm, w, 4),
    ]
    for copy in loads:
        copy.start()
    greet(s, core)
    greet(s, across)
    greet(mate, h)

    @pl.when(a < line - 1)
    def _():
        greet(s + 2, h)

    @pl.when(a > 0)
    def _():
        greet(s - 2, h)

    def spot(cond):
        return jnp.where(cond, 1, 0)

    docs_row = docs_ref[...].astype(F32)
    doc_col[...] = jnp.broadcast_to(docs_row, (dh, length)).T
    last_doc = doc_col[pl.ds(length - 1, 1), :]
    first_doc = doc_col[pl.ds(0, 1), :]
    tail[...] = jnp.where(doc_col[...] == last_doc, 1.0, 0.0).astype(BF)
    front[...] = jnp.where(doc_col[...] == first_doc, 1.0, 0.0).astype(BF)
    for c in range(pairs):
        f_own[c, pl.ds(rows, 16), :] = jnp.broadcast_to(last_doc, (16, dh)).astype(BF)
        r_own[c, pl.ds(rows, 16), :] = jnp.broadcast_to(first_doc, (16, dh)).astype(BF)

    def blank(ref):
        ref[...] = jnp.zeros_like(ref)
        for c in range(pairs):
            ref[c, pl.ds(rows, 16), :] = jnp.full((16, dh), -1.0, BF)

    @pl.when(a == 0)
    def _():
        blank(f_carry)

    @pl.when(a == line - 1)
    def _():
        blank(r_carry)

    pl.semaphore_wait(barrier, 3 + spot(a < line - 1) + spot(a > 0))

    loads[0].wait()
    theirs = pl.ds(pl.multiple_of((1 - b) * width, 128), width)
    ours = pl.ds(pl.multiple_of(b * width, 128), width)

    def g_part(slot, at, i, to):
        part_of = g.at[slot, at[0], at[1]]
        return remote(part_of, part_of, g_send.at[i], g_recv.at[i], s, to)

    whole = pl.ds(0, length)
    head_rows = 3 * length // 8
    slices = pl.ds(0, head_rows), pl.ds(head_rows, length - head_rows)
    g_core = g_part(h, (whole, pl.ds(0, share)), 0, core)
    g_ours = g_part(h, (whole, ours), 1, across)
    g_theirs = g_part(h, (whole, theirs), 2, across)
    g_pass_ours = g_part(across, (whole, ours), 3, core)
    g_pass_theirs = g_part(across, (whole, theirs), 4, core)
    p_mates = [
        remote(g.at[h, at, theirs], p.at[h, at, :], p_send.at[i], p_recv.at[i], mate, h)
        for i, at in enumerate(slices)
    ]
    p_acrosses = [
        remote(p.at[h, at, :], p.at[h, at, :], p_send.at[4 + i], p_recv.at[4 + i], s, across)
        for i, at in enumerate(slices)
    ]
    p_core = remote(p.at[h], p.at[h], p_send.at[2], p_recv.at[2], s, core)
    p_pass = remote(p.at[across], p.at[across], p_send.at[3], p_recv.at[3], s, core)
    g_ours.start()
    p_mates[0].start()
    g_core.start()

    class States:
        def __init__(self, split, sign, step, odd, own, mate_ref, after, carry, low, ss, rs):
            self.split, self.sign, self.step, self.odd = split, sign, step, odd
            self.own, self.mate, self.after, self.carry, self.low = own, mate_ref, after, carry, low
            self.ss, self.rs = ss, rs

        def swap(self, c):
            return remote(
                self.own.at[c], self.mate.at[c], self.ss.at[0, c], self.rs.at[0, c], mate, h
            )

        def onward(self, c):
            return remote(
                self.after.at[c], self.carry.at[c], self.ss.at[1, c], self.rs.at[1, c],
                s + self.sign * 2, h,
            )

        def values(self, ref, c):
            return (
                ref[c, pl.ds(0, rows), :].astype(F32),
                ref[c, pl.ds(rows, 1), :].astype(F32),
            )

        def add(self, base, more):
            same = jnp.broadcast_to(jnp.where(base[1] == more[1], 1.0, 0.0), (rows, dh))
            return base[0] + more[0] * same, base[1]

        def members(self, c):
            mine, other = self.values(self.own, c), self.values(self.mate, c)
            odd = self.odd == 1
            early = tuple(jnp.where(odd, y, x) for x, y in zip(mine, other))
            late = tuple(jnp.where(odd, x, y) for x, y in zip(mine, other))
            return early, late

        def forward(self, c):
            early, late = self.members(c)
            total, doc = self.add(self.add(late, early), self.values(self.carry, c))
            self.after[c, pl.ds(0, rows), :] = total.astype(BF)
            self.after[c, pl.ds(rows, 16), :] = jnp.broadcast_to(doc, (16, dh)).astype(BF)
            self.onward(c).start()

        def settle(self, c):
            early, _ = self.members(c)
            carry = self.values(self.carry, c)
            odd = self.odd == 1
            total = jnp.where(odd, self.add(early, carry)[0], carry[0]).astype(BF)
            self.low[2 * c] = total[:dh]
            self.low[2 * c + 1] = total[dh:]

        def open(self, c):
            self.swap(c).wait_recv()

            @pl.when((self.step == 0) & self.mine(c))
            def _():
                self.forward(c)

        def mine(self, c):
            return (c % 2 == b) if self.split else (c >= 0)

        def share(self, c):
            return remote(
                self.carry.at[c], self.carry.at[c], self.ss.at[2, c], self.rs.at[2, c], mate, h
            )

        def relay(self, c):
            @pl.when((self.step > 0) & self.mine(c))
            def _():
                self.onward(c).wait_recv()
                self.share(c).start()

                @pl.when(self.step < line - 1)
                def _():
                    self.forward(c)

        def shared(self, c):
            @pl.when((self.step > 0) & ~self.mine(c))
            def _():
                self.share(c).wait_recv()

        def serve(self, c):
            @pl.when((self.step > 0) & (c > 0))
            def _():
                self.onward(c).wait_recv()

            @pl.when((self.step > 0) & (self.step < line - 1))
            def _():
                self.forward(c)

            self.settle(c)

        def reached(self):
            early, _ = self.members(0)
            doc = jnp.where(self.odd == 1, early[1], self.values(self.carry, 0)[1])
            return jnp.where(doc_col[...] == doc, 1.0, 0.0)

        def drain(self, c):
            self.swap(c).wait_send()

            @pl.when((self.step < line - 1) & self.mine(c))
            def _():
                self.onward(c).wait_send()

            if self.split:
                @pl.when((self.step > 0) & self.mine(c))
                def _():
                    self.share(c).wait_send()

    ahead = States(False, 1, a, b, f_own, f_mate, f_next, f_carry, f_low, f_send, f_recv)
    behind = States(
        True, -1, line - 1 - a, 1 - b, r_own, r_mate, r_next, r_carry, r_low, r_send, r_recv
    )

    some = 64

    def by_head(raw, ref):
        def block(i):
            at = pl.ds(pl.multiple_of(i * some, some), some)
            ref[:, at, :] = jnp.swapaxes(raw[at], 0, 1)

        loop(length // some, block)

    def by_token(ref, raw):
        def block(i):
            at = pl.ds(pl.multiple_of(i * some, some), some)
            raw[at] = jnp.swapaxes(ref[:, at, :], 0, 1)

        loop(length // some, block)

    loads[1].wait()
    by_head(raw_k, k)
    loads[2].wait()
    by_head(raw_v, v)

    def own_state(c):
        for i in range(2):
            f_own[c, pl.ds(i * dh, dh), :] = dot_tn(
                k[2 * c + i] * tail[...], v[2 * c + i]
            ).astype(BF)
        ahead.swap(c).start()

    own_state(0)
    p_mates[1].start()
    loop(pairs - 1, lambda c: own_state(c + 1))
    p_mates[0].wait_recv()
    p_acrosses[0].start()
    loads[3].wait()
    by_head(raw_q, q)

    for i in range(length // dh):
        at = pl.ds(i * dh, dh)
        col = doc_col[at, :][:, :1]
        t_pos = lax.broadcasted_iota(jnp.int32, (dh, length), 0) + i * dh
        s_pos = lax.broadcasted_iota(jnp.int32, (dh, length), 1)
        ok = (t_pos >= s_pos) & (col == docs_row)
        mask[at, :] = jnp.where(ok, 1.0, 0.0).astype(BF)

    ahead.open(0)

    def local_attention(head):
        scores[head] = dot_nt(q[head], k[head]).astype(BF) * mask[...]
        attn[head] = dot_nn(scores[head], v[head])

    def between(low, high, body):
        lax.fori_loop(low, high, lambda i, _: (body(i), None)[1], None)

    def cotangents(pair, slot):
        return dot_nt(
            g[slot],
            w[pl.ds(pl.multiple_of(pair * tile, tile), tile), pl.ds(pl.multiple_of(slot * share, 128), share)],
        )

    def first_cotangents(pair):
        gn[pair] = cotangents(pair, h) + cotangents(pair, core)

    def hand_on():
        p_mates[1].wait_recv()
        p_acrosses[1].start()
        p_core.start()
        g_theirs.start()
        g_ours.wait_recv()
        g_pass_ours.start()
        loads[4].wait()
        g_core.wait_recv()

        @pl.when(a == line - 1)
        def _():
            loop(pairs, first_cotangents)

    def nt_copy(head):
        at = pl.ds(pl.multiple_of(head * dh, dh), dh)
        return remote(nt.at[at, :], ntp.at[at, :], n_send.at[head], n_recv.at[head], mate, h)

    def scale_of(value):
        return lax.rsqrt(jnp.mean(value * value, axis=-1, keepdims=True) + 1e-05)

    soon = jnp.where(at_end, 1, pairs // 2)

    def normalise(c):
        ahead.serve(c)
        for i in range(2):
            head = 2 * c + i
            value = attn[head] + reads[...] * dot_nn(q[head], f_low[head])
            attn[head] = value
            low = (value * scale_of(value)).astype(BF)
            at = pl.ds(pl.multiple_of(head * dh, dh), dh)
            normed[:, at] = low
            nt[at, :] = low.T

            @pl.when(c < soon)
            def _():
                nt_copy(head).start()

    late = a >= line // 2
    enough = jnp.where(late, heads, heads // 2)
    between(0, enough, local_attention)

    @pl.when(late)
    def _():
        hand_on()

    @pl.when(a > 0)
    def _():
        ahead.onward(0).wait_recv()

    reads[...] = ahead.reached()
    normalise(0)
    between(enough, heads, local_attention)

    @pl.when(~late)
    def _():
        hand_on()

    loop(pairs - 1, lambda c: ahead.open(c + 1))
    between(1, jnp.where(at_end, 1, pairs), normalise)

    @pl.when(a < line - 1)
    def _():
        loop(pairs, first_cotangents)

    for copy in p_acrosses:
        copy.wait_recv()
    p_pass.start()
    p_core.wait_recv()
    g_pass_ours.wait_recv()
    p_pass.wait_recv()

    def rest_of_cotangents():
        g_theirs.wait_recv()
        g_pass_theirs.start()
        g_pass_theirs.wait_recv()

    def grad_attention(c):
        pair_gn = gn[c] + cotangents(c, across) + cotangents(c, both)
        for i in range(2):
            head = 2 * c + i
            value = attn[head]
            scale = scale_of(value)
            norm = value * scale
            grad = pair_gn[:, i * dh : (i + 1) * dh]
            low = (scale * (grad - norm * jnp.mean(grad * norm, axis=-1, keepdims=True))).astype(BF)
            ga[head] = low
            r_own[c, pl.ds(i * dh, dh), :] = dot_tn(q[head] * front[...], low).astype(BF)
        behind.swap(c).start()

    def gradients():
        rest_of_cotangents()
        loop(pairs, grad_attention)
        between(2 * soon, heads, lambda head: nt_copy(head).start())

    def u_copy(d, j):
        at = pl.ds(pl.multiple_of(j * rows, rows), rows)
        return remote(sb.at[d, at, :], ub.at[d, at, :], u_ss.at[d, j], u_rs.at[d, j], s + 2, h)

    def d_copy(d, j):
        at = pl.ds(pl.multiple_of(j * rows, rows), rows)
        return remote(sb.at[d, at, :], db.at[d, at, :], d_ss.at[d, j], d_rs.at[d, j], s - 2, h)

    def weight_terms(first, count, low=0, high=line):
        if low == 0:
            for j in range(first, first + count):
                nt_copy(2 * j).wait_recv()
                nt_copy(2 * j + 1).wait_recv()

        def one(i):
            r = i // count
            j = first + i % count
            at = pl.ds(pl.multiple_of(j * rows, rows), rows)
            d = jnp.where(r % 2 == 0, line - 1 - r // 2, r // 2)
            d = jnp.where(a < line // 2, d, line - 1 - d)
            part[...] = dot_nn(nt[at, :], g[d, :, ours]) + dot_nn(ntp[at, :], p[d])

            @pl.when((d > a) & (a > 0))
            def _():
                u_copy(d, j).wait_recv()
                part[...] += ub[d, at, :].astype(F32)

            @pl.when((d < a) & (a < line - 1))
            def _():
                d_copy(d, j).wait_recv()
                part[...] += db[d, at, :].astype(F32)

            @pl.when(d == a)
            def _():
                gacc[at, :] = part[...]

            @pl.when(d != a)
            def _():
                sb[d, at, :] = part[...].astype(BF)

            @pl.when(d > a)
            def _():
                u_copy(d, j).start()

            @pl.when(d < a)
            def _():
                d_copy(d, j).start()

        between(low * count, high * count, one)

    @pl.when(~at_end)
    def _():
        gradients()

    weight_terms(0, 1)

    @pl.when(at_end)
    def _():
        between(1, pairs, normalise)
        gradients()

    loop(pairs, behind.open)

    @pl.when(at_end)
    def _():
        weight_terms(1, 1)

    tiles = share // tile

    def projected(d, t):
        at = pl.ds(pl.multiple_of(d * share + t * tile, 128), tile)
        return dot_nn(normed[...], w[:, at])

    def lc_copy(side):
        return remote(
            lc_send.at[side], lc_recv.at[side], lc_ss.at[side], lc_rs.at[side], s, core
        )

    lx_copy = remote(lx_send, lx_recv, lx_ss.at[0], lx_rs.at[0], s, across)

    def columns(t):
        return pl.ds(pl.multiple_of(t * tile, tile), tile)

    for side in (1 - hx, hx):
        def give(t, side=side):
            lc_send[side, :, columns(t)] = projected(2 * side + 1 - hc, t).astype(BF)

        loop(tiles, give)
        lc_copy(side).start()

    lc_copy(1 - hx).wait_recv()

    def cross(t):
        lx_send[:, columns(t)] = (
            projected(2 * (1 - hx) + hc, t) + lc_recv[1 - hx, :, columns(t)].astype(F32)
        ).astype(BF)

    loop(tiles, cross)
    lx_copy.start()

    def backward(c):
        for i in range(2):
            head = 2 * c + i
            grad = ga[head]
            gs = dot_nt(grad, v[head]).astype(BF) * mask[...]
            gq = dot_nn(gs, k[head]) + reads[...] * dot_nt(grad, f_low[head])
            attn[head] = dot_tn(gs, q[head])
            gn[c, :, pl.ds(i * dh, dh)] = dot_tn(scores[head], grad)
            q[head] = gq.astype(BF)

    def serve_back():
        loop(pairs, behind.relay)
        loop(pairs, behind.shared)
        writes[...] = behind.reached()
        loop(pairs, behind.settle)

    some_heads = jnp.where(at_end, 0, pairs // 2)
    between(0, some_heads, backward)

    @pl.when(~at_end)
    def _():
        serve_back()
        weight_terms(1, 1)

    @pl.when(at_end)
    def _():
        weight_terms(2, pairs - 2)

    between(some_heads, pairs, backward)

    @pl.when(~at_end)
    def _():
        weight_terms(2, pairs - 2, 0, 1)


    lc_copy(hx).wait_recv()

    def keep(t):
        lo_acc[:, columns(t)] = projected(h, t) + lc_recv[hx, :, columns(t)].astype(F32)

    loop(tiles, keep)

    by_token(q, raw_q)

    @pl.when(at_end)
    def _():
        serve_back()

    def backward_states(c):
        for i in range(2):
            head = 2 * c + i
            gk = attn[head] + writes[...] * dot_nt(v[head], r_low[head])
            gv = gn[c, :, pl.ds(i * dh, dh)] + writes[...] * dot_nn(k[head], r_low[head])
            k[head] = gk.astype(BF)
            v[head] = gv.astype(BF)

    loop(pairs, backward_states)
    by_token(k, raw_k)
    by_token(v, raw_v)

    @pl.when(~at_end)
    def _():
        weight_terms(2, pairs - 2, 1, line)

    lx_copy.wait_recv()
    lo_fin[...] = (lo_acc[...] + lx_recv[...].astype(F32)).astype(BF)

    def finish(j):
        at = pl.ds(pl.multiple_of(j * rows, rows), rows)

        @pl.when(a > 0)
        def _():
            u_copy(a, j).wait_recv()
            gacc[at, :] += ub[a, at, :].astype(F32)

        @pl.when(a < line - 1)
        def _():
            d_copy(a, j).wait_recv()
            gacc[at, :] += db[a, at, :].astype(F32)

    loop(pairs, finish)

    for copy in (
        g_core, g_ours, g_theirs, g_pass_ours, g_pass_theirs,
        *p_mates, *p_acrosses, p_core, p_pass, lx_copy,
    ):
        copy.wait_send()
    for side in range(2):
        lc_copy(side).wait_send()

    def drain(c):
        nt_copy(2 * c).wait_send()
        nt_copy(2 * c + 1).wait_send()
        ahead.drain(c)
        behind.drain(c)

        def lines(d):
            @pl.when(d > a)
            def _():
                u_copy(d, c).wait_send()

            @pl.when(d < a)
            def _():
                d_copy(d, c).wait_send()

        loop(line, lines)

    loop(pairs, drain)


def fused(queries, key_vectors, value_vectors, doc_ids, out_weight, grad_out):
    n = lax.axis_size("seq")
    m = lax.axis_size("head")
    length, heads, dh = queries.shape
    feats, columns = out_weight.shape
    share = columns // m
    width = columns // n
    line = n // 2
    pairs = heads // 2
    docs = doc_ids.reshape(1, length)
    vm = pltpu.VMEM
    heads_bf = vm((heads, length, dh), BF)
    state = vm((pairs, 2 * dh + 16, dh), BF)
    low = vm((heads, dh, dh), BF)
    terms = vm((line, feats, width), BF)
    dma = pltpu.SemaphoreType.DMA
    scratch = [
        heads_bf, heads_bf, heads_bf,
        vm((feats, columns), BF),
        vm((m, length, share), BF),
        vm((m, length, width), BF),
        vm((length, length), BF),
        vm((heads, length, length), BF),
        vm((heads, length, dh), F32),
        vm((pairs, length, 2 * dh), F32),
        vm((length, feats), BF),
        vm((feats, length), BF),
        vm((feats, length), BF),
        heads_bf,
        state, state, state, state, low,
        state, state, state, state, low,
        vm((2, length, share), BF), vm((2, length, share), BF),
        vm((length, share), BF), vm((length, share), BF),
        vm((length, share), F32),
        terms, terms, terms,
        vm((2 * dh, width), F32),
        vm((length, dh), F32), vm((length, dh), F32), vm((length, dh), F32),
        vm((length, dh), BF), vm((length, dh), BF),
        dma((5,)), dma((5,)), dma((5,)), dma((6,)), dma((6,)),
        dma((2, pairs)), dma((2, pairs)), dma((3, pairs)), dma((3, pairs)),
        dma((heads,)), dma((heads,)), dma((2,)), dma((2,)), dma((1,)), dma((1,)),
        dma((line, pairs)), dma((line, pairs)), dma((line, pairs)), dma((line, pairs)),
    ]
    anywhere = pl.BlockSpec(memory_space=pl.ANY)
    grads = pltpu.VMEM((length, heads, dh), BF)
    lo, gq, gk, gv, gw = pl.pallas_call(
        functools.partial(kernel, (n, m, heads, length, dh, share, width)),
        out_shape=(
            pltpu.VMEM((length, share), BF), grads, grads, grads,
            pltpu.VMEM((feats, width), F32),
        ),
        in_specs=[pl.BlockSpec(memory_space=pltpu.VMEM)] + [anywhere] * 5,
        out_specs=(pl.BlockSpec(memory_space=pltpu.VMEM),) * 5,
        scratch_shapes=scratch,
        compiler_params=pltpu.CompilerParams(
            collective_id=0, has_side_effects=True, vmem_limit_bytes=54 << 20
        ),
    )(docs, queries, key_vectors, value_vectors, out_weight, grad_out)
    return lo, gq, gk, gv, gw


def shift(block, distance):
    n = lax.axis_size("seq")
    route = [(i, i + distance) for i in range(n) if 0 <= i + distance < n]
    return lax.ppermute(block, "seq", route)


def swap(block, axis, bit):
    n = lax.axis_size(axis)
    return lax.ppermute(block, axis, [(i, i ^ bit) for i in range(n)])


def gather_heads(block, first):
    me = lax.axis_index("head")
    bit = lax.axis_size("head") // 2
    columns = block.shape[1]
    held = [block]
    while bit:
        other = swap(jnp.concatenate(held, axis=1), "head", bit)
        if first is not None:
            other, first = lax.optimization_barrier((other, first))
            first = None
        high = (me // bit) % 2 == 1
        merged = []
        for i, own in enumerate(held):
            theirs = other[:, i * columns : (i + 1) * columns]
            merged += [jnp.where(high, theirs, own), jnp.where(high, own, theirs)]
        held = merged
        bit //= 2
    return held


def scatter_heads(partial):
    me = lax.axis_index("head")
    size = lax.axis_size("head")
    share = partial.shape[1] // size
    held = [partial[:, i * share : (i + 1) * share] for i in range(size)]
    bit = 1
    while bit < size:
        high = (me // bit) % 2 == 1
        couples = list(zip(held[0::2], held[1::2]))
        given = jnp.concatenate([jnp.where(high, a, b).astype(BF) for a, b in couples], axis=1)
        other = swap(given, "head", bit)
        held = [
            jnp.where(high, b, a) + other[:, i * share : (i + 1) * share].astype(F32)
            for i, (a, b) in enumerate(couples)
        ]
        bit *= 2
    return held[0].astype(BF)


def with_doc(state, doc):
    rows = jnp.broadcast_to(doc.astype(BF)[:, None], (16, state.shape[-1]))
    return jnp.concatenate([state.astype(BF).reshape(-1, state.shape[-1]), rows], axis=0)


def window(total, sign, first=None):
    rows = lax.broadcasted_iota(jnp.int32, (total.shape[0], 1), 0) < total.shape[0] - 16
    span = 1
    while span < lax.axis_size("seq") // 2:
        far = shift(total, sign * span)
        if first is not None and 4 * span >= lax.axis_size("seq"):
            far, first = lax.optimization_barrier((far, first))
        same = (far[-16:-15] == total[-16:-15]) & rows
        total = total + jnp.where(same, far, jnp.zeros_like(far))
        span *= 2
    return total


def plain(queries, key_vectors, value_vectors, doc_ids, out_weight, grad_out):
    n = lax.axis_size("seq")
    m = lax.axis_size("head")
    length, heads, dh = queries.shape
    place = lax.axis_index("seq")
    parity = place % 2
    line = n // 2
    where_on_line = place // 2
    columns = out_weight.shape[1]
    width = columns // n

    docs = doc_ids.astype(F32)
    tail = (docs == docs[-1]).astype(BF)
    own_state = jnp.einsum(
        "shd,she->hde", key_vectors * tail[:, None, None], value_vectors, preferred_element_type=F32
    )
    near_flat = shift(with_doc(own_state, docs[-1:]), 1)
    own_gathered = gather_heads(grad_out, near_flat)
    near_flat, grad_out = lax.optimization_barrier((near_flat, grad_out))
    flat = window(near_flat, 1)
    before = flat[-16, :1].astype(F32)
    state_low = flat[:-16].reshape(own_state.shape)

    causal = lax.broadcasted_iota(jnp.int32, (length, length), 0) >= lax.broadcasted_iota(
        jnp.int32, (length, length), 1
    )
    pairs = causal & (docs[:, None] == docs[None, :])
    reads = (docs == before[0]).astype(F32)
    scores = jnp.einsum("thd,shd->hts", queries, key_vectors, preferred_element_type=F32)
    scores_low = jnp.where(pairs[None], scores, 0.0).astype(BF)
    attn = jnp.einsum("hts,she->the", scores_low, value_vectors, preferred_element_type=F32)
    attn = attn + reads[:, None, None] * jnp.einsum(
        "thd,hde->the", queries, state_low, preferred_element_type=F32
    )
    scale = lax.rsqrt(jnp.mean(attn * attn, axis=-1, keepdims=True) + 1e-05)
    normed_f = attn * scale
    normed = normed_f.astype(BF).reshape(length, -1)
    partner_normed = swap(normed, "seq", 1)

    share = columns // m
    odd = parity == 1
    for_partner = [
        jnp.where(odd, grad_out[:, i : i + width], grad_out[:, i + width : i + 2 * width])
        for i in range(0, share, 2 * width)
    ]
    from_partner = swap(jnp.concatenate(for_partner, axis=1), "seq", 1)
    cotangent = jnp.concatenate(own_gathered, axis=1)
    partner_cot = jnp.concatenate(gather_heads(from_partner, normed), axis=1)

    grad_normed = lax.dot_general(
        cotangent, out_weight, (((1,), (1,)), ((), ())), preferred_element_type=F32
    ).reshape(attn.shape)
    grad_attn = (
        scale * (grad_normed - normed_f * jnp.mean(grad_normed * normed_f, axis=-1, keepdims=True))
    ).astype(BF)
    head_mask = (docs == docs[0]).astype(BF)
    own_back = jnp.einsum(
        "thd,the->hde", queries * head_mask[:, None, None], grad_attn, preferred_element_type=F32
    )
    near_flat = shift(with_doc(own_back, docs[:1]), -1)

    def share_of(step):
        goal = (where_on_line + step) % line
        mine = lax.dynamic_slice_in_dim(cotangent, (2 * goal + parity) * width, width, 1)
        theirs = lax.dynamic_slice_in_dim(partner_cot, goal * width, width, 1)
        over_tokens = (((0,), (0,)), ((), ()))
        return lax.dot_general(
            normed, mine, over_tokens, preferred_element_type=F32
        ) + lax.dot_general(partner_normed, theirs, over_tokens, preferred_element_type=F32)

    terms = [share_of(step).astype(BF) for step in range(1, line)]
    terms, near_flat = lax.optimization_barrier((terms, near_flat))
    terms, grad_attn_in, normed_out = lax.optimization_barrier((terms, grad_attn, normed))
    partial_out = jnp.dot(normed_out, out_weight, preferred_element_type=F32)
    layer_out = scatter_heads(partial_out)
    flat = window(near_flat, -1, layer_out)
    after = flat[-16, :1].astype(F32)
    back_low = flat[:-16].reshape(own_back.shape)
    writes = (docs == after[0]).astype(F32)
    arrived = []
    for step, term in enumerate(terms, 1):
        route = [
            (2 * a + b, 2 * ((a + step) % line) + b) for a in range(line) for b in range(2)
        ]
        arrived.append(lax.ppermute(term, "seq", route))
    own_term = share_of(0)

    grad_scores = jnp.einsum("the,she->hts", grad_attn_in, value_vectors, preferred_element_type=F32)
    grad_scores = jnp.where(pairs[None], grad_scores, 0.0).astype(BF)
    grad_queries = jnp.einsum("hts,shd->thd", grad_scores, key_vectors, preferred_element_type=F32)
    grad_queries = grad_queries + reads[:, None, None] * jnp.einsum(
        "the,hde->thd", grad_attn_in, state_low, preferred_element_type=F32
    )
    grad_keys = jnp.einsum("hts,thd->shd", grad_scores, queries, preferred_element_type=F32)
    grad_keys = grad_keys + writes[:, None, None] * jnp.einsum(
        "she,hde->shd", value_vectors, back_low, preferred_element_type=F32
    )
    grad_values = jnp.einsum("hts,the->she", scores_low, grad_attn_in, preferred_element_type=F32)
    grad_values = grad_values + writes[:, None, None] * jnp.einsum(
        "shd,hde->she", key_vectors, back_low, preferred_element_type=F32
    )
    arrived, layer_out = lax.optimization_barrier((arrived, layer_out))
    grad_weight = own_term
    for part in arrived:
        grad_weight = grad_weight + part.astype(F32)
    return (
        layer_out,
        grad_queries.astype(BF),
        grad_keys.astype(BF),
        grad_values.astype(BF),
        grad_weight,
    )


def fits(mesh, columns, heads, dh):
    n, m = mesh.shape["seq"], mesh.shape["head"]
    return m == 4 and n == 2 * m and columns % (128 * n) == 0 and heads == 8 and dh == 128


def choose(mesh):
    def shards(queries, key_vectors, value_vectors, doc_ids, out_weight, grad_out):
        heads, dh = queries.shape[1:]
        form = fused if fits(mesh, out_weight.shape[1], heads, dh) else plain
        return form(queries, key_vectors, value_vectors, doc_ids, out_weight, grad_out)

    return shards


def solution(mesh):
    placed = (
        P("seq", "head", None),
        P("seq", "head", None),
        P("seq", "head", None),
        P("seq"),
        P("head", None),
        P("seq", "head"),
    )
    return jax.shard_map(
        choose(mesh),
        mesh=mesh,
        in_specs=placed,
        out_specs=(
            P("seq", "head"),
            P("seq", "head", None),
            P("seq", "head", None),
            P("seq", "head", None),
            P("head", "seq"),
        ),
        check_vma=False,
    )
```

```python
import functools

import jax
import jax.numpy as jnp
from jax import lax
from jax.experimental import pallas as pl
from jax.experimental.pallas import tpu as pltpu
from jax.sharding import PartitionSpec as P


BF = jnp.bfloat16
F32 = jnp.float32
MESH = pl.DeviceIdType.MESH


def dot_nn(a, b):
    return lax.dot_general(a, b, (((1,), (0,)), ((), ())), preferred_element_type=F32)


def dot_nt(a, b):
    return lax.dot_general(a, b, (((1,), (1,)), ((), ())), preferred_element_type=F32)


def dot_tn(a, b):
    return lax.dot_general(a, b, (((0,), (0,)), ((), ())), preferred_element_type=F32)


def loop(count, body):
    lax.fori_loop(0, count, lambda i, _: (body(i), None)[1], None)


def kernel(
    sizes,
    docs_ref, q_hbm, k_hbm, v_hbm, w_hbm, go_hbm,
    lo_fin, raw_q, raw_k, raw_v, gacc,
    q, k, v, w, g, p, mask, scores, attn, gn, normed, nt, ntp, ga,
    f_own, f_mate, f_next, f_carry, f_low,
    r_own, r_mate, r_next, r_carry, r_low,
    lc_send, lc_recv, lx_send, lx_recv, lo_acc,
    sb, ub, db, part,
    doc_col, reads, writes, tail, front,
    in_sem, g_send, g_recv, p_send, p_recv, f_send, f_recv, r_send, r_recv,
    n_send, n_recv, lc_ss, lc_rs, lx_ss, lx_rs, u_ss, u_rs, d_ss, d_rs,
):
    n, m, heads, length, dh, share, width = sizes
    line = n // 2
    pairs = heads // 2
    rows = 2 * dh
    tile = 2 * dh
    s = lax.axis_index("seq")
    h = lax.axis_index("head")
    a = s // 2
    b = s % 2
    hc = h % 2
    hx = h // 2
    core = h + 1 - 2 * hc
    across = h + 2 - 4 * hx
    both = core + 2 - 4 * hx
    mate = s + 1 - 2 * b
    at_end = (a == 0) | (a == line - 1)

    barrier = pltpu.get_barrier_semaphore()

    def greet(seq, head):
        pl.semaphore_signal(barrier, inc=1, device_id=(seq, head), device_id_type=MESH)

    def local(src, dst, i):
        return pltpu.make_async_copy(src, dst, in_sem.at[i])

    def remote(src, dst, ss, rs, seq, head):
        return pltpu.make_async_remote_copy(
            src_ref=src, dst_ref=dst, send_sem=ss, recv_sem=rs,
            device_id=(seq, head), device_id_type=MESH,
        )

    loads = [
        local(go_hbm, g.at[h], 0), local(k_hbm, raw_k, 1), local(v_hbm, raw_v, 2),
        local(q_hbm, raw_q, 3), local(w_hbm, w, 4),
    ]
    for copy in loads:
        copy.start()
    greet(s, core)
    greet(s, across)
    greet(mate, h)

    @pl.when(a < line - 1)
    def _():
        greet(s + 2, h)

    @pl.when(a > 0)
    def _():
        greet(s - 2, h)

    def spot(cond):
        return jnp.where(cond, 1, 0)

    docs_row = docs_ref[...].astype(F32)
    doc_col[...] = jnp.broadcast_to(docs_row, (dh, length)).T
    last_doc = doc_col[pl.ds(length - 1, 1), :]
    first_doc = doc_col[pl.ds(0, 1), :]
    tail[...] = jnp.where(doc_col[...] == last_doc, 1.0, 0.0).astype(BF)
    front[...] = jnp.where(doc_col[...] == first_doc, 1.0, 0.0).astype(BF)
    for c in range(pairs):
        f_own[c, pl.ds(rows, 16), :] = jnp.broadcast_to(last_doc, (16, dh)).astype(BF)
        r_own[c, pl.ds(rows, 16), :] = jnp.broadcast_to(first_doc, (16, dh)).astype(BF)

    def blank(ref):
        ref[...] = jnp.zeros_like(ref)
        for c in range(pairs):
            ref[c, pl.ds(rows, 16), :] = jnp.full((16, dh), -1.0, BF)

    @pl.when(a == 0)
    def _():
        blank(f_carry)

    @pl.when(a == line - 1)
    def _():
        blank(r_carry)

    pl.semaphore_wait(barrier, 3 + spot(a < line - 1) + spot(a > 0))

    loads[0].wait()
    theirs = pl.ds(pl.multiple_of((1 - b) * width, 128), width)
    ours = pl.ds(pl.multiple_of(b * width, 128), width)

    def g_part(slot, at, i, to):
        part_of = g.at[slot, at[0], at[1]]
        return remote(part_of, part_of, g_send.at[i], g_recv.at[i], s, to)

    whole = pl.ds(0, length)
    head_rows = 3 * length // 8
    slices = pl.ds(0, head_rows), pl.ds(head_rows, length - head_rows)
    g_core = g_part(h, (whole, pl.ds(0, share)), 0, core)
    g_ours = g_part(h, (whole, ours), 1, across)
    g_theirs = g_part(h, (whole, theirs), 2, across)
    g_pass_ours = g_part(across, (whole, ours), 3, core)
    g_pass_theirs = g_part(across, (whole, theirs), 4, core)
    p_mates = [
        remote(g.at[h, at, theirs], p.at[h, at, :], p_send.at[i], p_recv.at[i], mate, h)
        for i, at in enumerate(slices)
    ]
    p_acrosses = [
        remote(p.at[h, at, :], p.at[h, at, :], p_send.at[4 + i], p_recv.at[4 + i], s, across)
        for i, at in enumerate(slices)
    ]
    p_core = remote(p.at[h], p.at[h], p_send.at[2], p_recv.at[2], s, core)
    p_pass = remote(p.at[across], p.at[across], p_send.at[3], p_recv.at[3], s, core)
    g_ours.start()
    p_mates[0].start()
    g_core.start()

    class States:
        def __init__(self, split, sign, step, odd, own, mate_ref, after, carry, low, ss, rs):
            self.split, self.sign, self.step, self.odd = split, sign, step, odd
            self.own, self.mate, self.after, self.carry, self.low = own, mate_ref, after, carry, low
            self.ss, self.rs = ss, rs

        def swap(self, c):
            return remote(
                self.own.at[c], self.mate.at[c], self.ss.at[0, c], self.rs.at[0, c], mate, h
            )

        def onward(self, c):
            return remote(
                self.after.at[c], self.carry.at[c], self.ss.at[1, c], self.rs.at[1, c],
                s + self.sign * 2, h,
            )

        def values(self, ref, c):
            return (
                ref[c, pl.ds(0, rows), :].astype(F32),
                ref[c, pl.ds(rows, 1), :].astype(F32),
            )

        def add(self, base, more):
            same = jnp.broadcast_to(jnp.where(base[1] == more[1], 1.0, 0.0), (rows, dh))
            return base[0] + more[0] * same, base[1]

        def members(self, c):
            mine, other = self.values(self.own, c), self.values(self.mate, c)
            odd = self.odd == 1
            early = tuple(jnp.where(odd, y, x) for x, y in zip(mine, other))
            late = tuple(jnp.where(odd, x, y) for x, y in zip(mine, other))
            return early, late

        def forward(self, c):
            early, late = self.members(c)
            total, doc = self.add(self.add(late, early), self.values(self.carry, c))
            self.after[c, pl.ds(0, rows), :] = total.astype(BF)
            self.after[c, pl.ds(rows, 16), :] = jnp.broadcast_to(doc, (16, dh)).astype(BF)
            self.onward(c).start()

        def settle(self, c):
            early, _ = self.members(c)
            carry = self.values(self.carry, c)
            odd = self.odd == 1
            total = jnp.where(odd, self.add(early, carry)[0], carry[0]).astype(BF)
            self.low[2 * c] = total[:dh]
            self.low[2 * c + 1] = total[dh:]

        def open(self, c):
            self.swap(c).wait_recv()

            @pl.when((self.step == 0) & self.mine(c))
            def _():
                self.forward(c)

        def mine(self, c):
            return (c % 2 == b) if self.split else (c >= 0)

        def share(self, c):
            return remote(
                self.carry.at[c], self.carry.at[c], self.ss.at[2, c], self.rs.at[2, c], mate, h
            )

        def relay(self, c):
            @pl.when((self.step > 0) & self.mine(c))
            def _():
                self.onward(c).wait_recv()
                self.share(c).start()

                @pl.when(self.step < line - 1)
                def _():
                    self.forward(c)

        def shared(self, c):
            @pl.when((self.step > 0) & ~self.mine(c))
            def _():
                self.share(c).wait_recv()

        def serve(self, c):
            @pl.when((self.step > 0) & (c > 0))
            def _():
                self.onward(c).wait_recv()

            @pl.when((self.step > 0) & (self.step < line - 1))
            def _():
                self.forward(c)

            self.settle(c)

        def reached(self):
            early, _ = self.members(0)
            doc = jnp.where(self.odd == 1, early[1], self.values(self.carry, 0)[1])
            return jnp.where(doc_col[...] == doc, 1.0, 0.0)

        def drain(self, c):
            self.swap(c).wait_send()

            @pl.when((self.step < line - 1) & self.mine(c))
            def _():
                self.onward(c).wait_send()

            if self.split:
                @pl.when((self.step > 0) & self.mine(c))
                def _():
                    self.share(c).wait_send()

    ahead = States(False, 1, a, b, f_own, f_mate, f_next, f_carry, f_low, f_send, f_recv)
    behind = States(
        True, -1, line - 1 - a, 1 - b, r_own, r_mate, r_next, r_carry, r_low, r_send, r_recv
    )

    some = 64

    def by_head(raw, ref):
        def block(i):
            at = pl.ds(pl.multiple_of(i * some, some), some)
            ref[:, at, :] = jnp.swapaxes(raw[at], 0, 1)

        loop(length // some, block)

    def by_token(ref, raw):
        def block(i):
            at = pl.ds(pl.multiple_of(i * some, some), some)
            raw[at] = jnp.swapaxes(ref[:, at, :], 0, 1)

        loop(length // some, block)

    loads[1].wait()
    by_head(raw_k, k)
    loads[2].wait()
    by_head(raw_v, v)

    def own_state(c):
        for i in range(2):
            f_own[c, pl.ds(i * dh, dh), :] = dot_tn(
                k[2 * c + i] * tail[...], v[2 * c + i]
            ).astype(BF)
        ahead.swap(c).start()

    own_state(0)
    p_mates[1].start()
    loop(pairs - 1, lambda c: own_state(c + 1))
    p_mates[0].wait_recv()
    p_acrosses[0].start()
    loads[3].wait()
    by_head(raw_q, q)

    for i in range(length // dh):
        at = pl.ds(i * dh, dh)
        col = doc_col[at, :][:, :1]
        t_pos = lax.broadcasted_iota(jnp.int32, (dh, length), 0) + i * dh
        s_pos = lax.broadcasted_iota(jnp.int32, (dh, length), 1)
        ok = (t_pos >= s_pos) & (col == docs_row)
        mask[at, :] = jnp.where(ok, 1.0, 0.0).astype(BF)

    ahead.open(0)

    def local_attention(head):
        scores[head] = dot_nt(q[head], k[head]).astype(BF) * mask[...]
        attn[head] = dot_nn(scores[head], v[head])

    def between(low, high, body):
        lax.fori_loop(low, high, lambda i, _: (body(i), None)[1], None)

    def cotangents(pair, slot):
        return dot_nt(
            g[slot],
            w[pl.ds(pl.multiple_of(pair * tile, tile), tile), pl.ds(pl.multiple_of(slot * share, 128), share)],
        )

    def first_cotangents(pair):
        gn[pair] = cotangents(pair, h) + cotangents(pair, core)

    def hand_on():
        p_mates[1].wait_recv()
        p_acrosses[1].start()
        p_core.start()
        g_theirs.start()
        g_ours.wait_recv()
        g_pass_ours.start()
        loads[4].wait()
        g_core.wait_recv()

        @pl.when(a == line - 1)
        def _():
            loop(pairs, first_cotangents)

    def nt_copy(head):
        at = pl.ds(pl.multiple_of(head * dh, dh), dh)
        return remote(nt.at[at, :], ntp.at[at, :], n_send.at[head], n_recv.at[head], mate, h)

    def scale_of(value):
        return lax.rsqrt(jnp.mean(value * value, axis=-1, keepdims=True) + 1e-05)

    soon = jnp.where(at_end, 1, pairs // 2)

    def normalise(c):
        ahead.serve(c)
        for i in range(2):
            head = 2 * c + i
            value = attn[head] + reads[...] * dot_nn(q[head], f_low[head])
            attn[head] = value
            low = (value * scale_of(value)).astype(BF)
            at = pl.ds(pl.multiple_of(head * dh, dh), dh)
            normed[:, at] = low
            nt[at, :] = low.T

            @pl.when(c < soon)
            def _():
                nt_copy(head).start()

    late = a >= line // 2
    enough = jnp.where(late, heads, heads // 2)
    between(0, enough, local_attention)

    @pl.when(late)
    def _():
        hand_on()

    @pl.when(a > 0)
    def _():
        ahead.onward(0).wait_recv()

    reads[...] = ahead.reached()
    normalise(0)
    between(enough, heads, local_attention)

    @pl.when(~late)
    def _():
        hand_on()

    loop(pairs - 1, lambda c: ahead.open(c + 1))
    between(1, jnp.where(at_end, 1, pairs), normalise)

    @pl.when(a < line - 1)
    def _():
        loop(pairs, first_cotangents)

    for copy in p_acrosses:
        copy.wait_recv()
    p_pass.start()
    p_core.wait_recv()
    g_pass_ours.wait_recv()
    p_pass.wait_recv()

    def rest_of_cotangents():
        g_theirs.wait_recv()
        g_pass_theirs.start()
        g_pass_theirs.wait_recv()

    def grad_attention(c):
        pair_gn = gn[c] + cotangents(c, across) + cotangents(c, both)
        for i in range(2):
            head = 2 * c + i
            value = attn[head]
            scale = scale_of(value)
            norm = value * scale
            grad = pair_gn[:, i * dh : (i + 1) * dh]
            low = (scale * (grad - norm * jnp.mean(grad * norm, axis=-1, keepdims=True))).astype(BF)
            ga[head] = low
            r_own[c, pl.ds(i * dh, dh), :] = dot_tn(q[head] * front[...], low).astype(BF)
        behind.swap(c).start()

    def gradients():
        rest_of_cotangents()
        loop(pairs, grad_attention)
        between(2 * soon, heads, lambda head: nt_copy(head).start())

    def u_copy(d, j):
        at = pl.ds(pl.multiple_of(j * rows, rows), rows)
        return remote(sb.at[d, at, :], ub.at[d, at, :], u_ss.at[d, j], u_rs.at[d, j], s + 2, h)

    def d_copy(d, j):
        at = pl.ds(pl.multiple_of(j * rows, rows), rows)
        return remote(sb.at[d, at, :], db.at[d, at, :], d_ss.at[d, j], d_rs.at[d, j], s - 2, h)

    def weight_terms(first, count, low=0, high=line):
        if low == 0:
            for j in range(first, first + count):
                nt_copy(2 * j).wait_recv()
                nt_copy(2 * j + 1).wait_recv()

        def one(i):
            r = i // count
            j = first + i % count
            at = pl.ds(pl.multiple_of(j * rows, rows), rows)
            d = jnp.where(r % 2 == 0, line - 1 - r // 2, r // 2)
            d = jnp.where(a < line // 2, d, line - 1 - d)
            part[...] = dot_nn(nt[at, :], g[d, :, ours]) + dot_nn(ntp[at, :], p[d])

            @pl.when((d > a) & (a > 0))
            def _():
                u_copy(d, j).wait_recv()
                part[...] += ub[d, at, :].astype(F32)

            @pl.when((d < a) & (a < line - 1))
            def _():
                d_copy(d, j).wait_recv()
                part[...] += db[d, at, :].astype(F32)

            @pl.when(d == a)
            def _():
                gacc[at, :] = part[...]

            @pl.when(d != a)
            def _():
                sb[d, at, :] = part[...].astype(BF)

            @pl.when(d > a)
            def _():
                u_copy(d, j).start()

            @pl.when(d < a)
            def _():
                d_copy(d, j).start()

        between(low * count, high * count, one)

    @pl.when(~at_end)
    def _():
        gradients()

    weight_terms(0, 1)

    @pl.when(at_end)
    def _():
        between(1, pairs, normalise)
        gradients()

    loop(pairs, behind.open)

    @pl.when(at_end)
    def _():
        weight_terms(1, 1)

    tiles = share // tile

    def projected(d, t):
        at = pl.ds(pl.multiple_of(d * share + t * tile, 128), tile)
        return dot_nn(normed[...], w[:, at])

    def lc_copy(side):
        return remote(
            lc_send.at[side], lc_recv.at[side], lc_ss.at[side], lc_rs.at[side], s, core
        )

    lx_copy = remote(lx_send, lx_recv, lx_ss.at[0], lx_rs.at[0], s, across)

    def columns(t):
        return pl.ds(pl.multiple_of(t * tile, tile), tile)

    for side in (1 - hx, hx):
        def give(t, side=side):
            lc_send[side, :, columns(t)] = projected(2 * side + 1 - hc, t).astype(BF)

        loop(tiles, give)
        lc_copy(side).start()

    lc_copy(1 - hx).wait_recv()

    def cross(t):
        lx_send[:, columns(t)] = (
            projected(2 * (1 - hx) + hc, t) + lc_recv[1 - hx, :, columns(t)].astype(F32)
        ).astype(BF)

    loop(tiles, cross)
    lx_copy.start()

    def backward(c):
        for i in range(2):
            head = 2 * c + i
            grad = ga[head]
            gs = dot_nt(grad, v[head]).astype(BF) * mask[...]
            gq = dot_nn(gs, k[head]) + reads[...] * dot_nt(grad, f_low[head])
            attn[head] = dot_tn(gs, q[head])
            gn[c, :, pl.ds(i * dh, dh)] = dot_tn(scores[head], grad)
            q[head] = gq.astype(BF)

    def serve_back():
        loop(pairs, behind.relay)
        loop(pairs, behind.shared)
        writes[...] = behind.reached()
        loop(pairs, behind.settle)

    some_heads = jnp.where(at_end, 0, pairs // 2)
    between(0, some_heads, backward)

    @pl.when(~at_end)
    def _():
        serve_back()
        weight_terms(1, 1)

    @pl.when(at_end)
    def _():
        weight_terms(2, pairs - 2)

    between(some_heads, pairs, backward)

    @pl.when(~at_end)
    def _():
        weight_terms(2, pairs - 2, 0, 1)


    lc_copy(hx).wait_recv()

    def keep(t):
        lo_acc[:, columns(t)] = projected(h, t) + lc_recv[hx, :, columns(t)].astype(F32)

    loop(tiles, keep)

    by_token(q, raw_q)

    @pl.when(at_end)
    def _():
        serve_back()

    def backward_states(c):
        for i in range(2):
            head = 2 * c + i
            gk = attn[head] + writes[...] * dot_nt(v[head], r_low[head])
            gv = gn[c, :, pl.ds(i * dh, dh)] + writes[...] * dot_nn(k[head], r_low[head])
            k[head] = gk.astype(BF)
            v[head] = gv.astype(BF)

    loop(pairs, backward_states)
    by_token(k, raw_k)
    by_token(v, raw_v)

    @pl.when(~at_end)
    def _():
        weight_terms(2, pairs - 2, 1, line)

    lx_copy.wait_recv()
    lo_fin[...] = (lo_acc[...] + lx_recv[...].astype(F32)).astype(BF)

    def finish(j):
        at = pl.ds(pl.multiple_of(j * rows, rows), rows)

        @pl.when(a > 0)
        def _():
            u_copy(a, j).wait_recv()
            gacc[at, :] += ub[a, at, :].astype(F32)

        @pl.when(a < line - 1)
        def _():
            d_copy(a, j).wait_recv()
            gacc[at, :] += db[a, at, :].astype(F32)

    loop(pairs, finish)

    for copy in (
        g_core, g_ours, g_theirs, g_pass_ours, g_pass_theirs,
        *p_mates, *p_acrosses, p_core, p_pass, lx_copy,
    ):
        copy.wait_send()
    for side in range(2):
        lc_copy(side).wait_send()

    def drain(c):
        nt_copy(2 * c).wait_send()
        nt_copy(2 * c + 1).wait_send()
        ahead.drain(c)
        behind.drain(c)

        def lines(d):
            @pl.when(d > a)
            def _():
                u_copy(d, c).wait_send()

            @pl.when(d < a)
            def _():
                d_copy(d, c).wait_send()

        loop(line, lines)

    loop(pairs, drain)


def put_out(*refs):
    count = len(refs) // 2
    copies = [
        pltpu.make_async_copy(refs[i], refs[count + i], refs[-1].at[i]) for i in range(count)
    ]
    for copy in copies:
        copy.start()
    for copy in copies:
        copy.wait()


def fused(queries, key_vectors, value_vectors, doc_ids, out_weight, grad_out):
    n = lax.axis_size("seq")
    m = lax.axis_size("head")
    length, heads, dh = queries.shape
    feats, columns = out_weight.shape
    share = columns // m
    width = columns // n
    line = n // 2
    pairs = heads // 2
    docs = doc_ids.reshape(1, length)
    vm = pltpu.VMEM
    heads_bf = vm((heads, length, dh), BF)
    state = vm((pairs, 2 * dh + 16, dh), BF)
    low = vm((heads, dh, dh), BF)
    terms = vm((line, feats, width), BF)
    dma = pltpu.SemaphoreType.DMA
    scratch = [
        heads_bf, heads_bf, heads_bf,
        vm((feats, columns), BF),
        vm((m, length, share), BF),
        vm((m, length, width), BF),
        vm((length, length), BF),
        vm((heads, length, length), BF),
        vm((heads, length, dh), F32),
        vm((pairs, length, 2 * dh), F32),
        vm((length, feats), BF),
        vm((feats, length), BF),
        vm((feats, length), BF),
        heads_bf,
        state, state, state, state, low,
        state, state, state, state, low,
        vm((2, length, share), BF), vm((2, length, share), BF),
        vm((length, share), BF), vm((length, share), BF),
        vm((length, share), F32),
        terms, terms, terms,
        vm((2 * dh, width), F32),
        vm((length, dh), F32), vm((length, dh), F32), vm((length, dh), F32),
        vm((length, dh), BF), vm((length, dh), BF),
        dma((5,)), dma((5,)), dma((5,)), dma((6,)), dma((6,)),
        dma((2, pairs)), dma((2, pairs)), dma((3, pairs)), dma((3, pairs)),
        dma((heads,)), dma((heads,)), dma((2,)), dma((2,)), dma((1,)), dma((1,)),
        dma((line, pairs)), dma((line, pairs)), dma((line, pairs)), dma((line, pairs)),
    ]
    anywhere = pl.BlockSpec(memory_space=pl.ANY)
    grads = pltpu.VMEM((length, heads, dh), BF)
    lo, gq, gk, gv, gw = pl.pallas_call(
        functools.partial(kernel, (n, m, heads, length, dh, share, width)),
        out_shape=(
            pltpu.VMEM((length, share), BF), grads, grads, grads,
            pltpu.VMEM((feats, width), F32),
        ),
        in_specs=[pl.BlockSpec(memory_space=pltpu.VMEM)] + [anywhere] * 5,
        out_specs=(pl.BlockSpec(memory_space=pltpu.VMEM),) * 5,
        scratch_shapes=scratch,
        compiler_params=pltpu.CompilerParams(
            collective_id=0, has_side_effects=True, vmem_limit_bytes=54 << 20
        ),
    )(docs, queries, key_vectors, value_vectors, out_weight, grad_out)
    results = lo, gq, gk, gv, gw
    return pl.pallas_call(
        put_out,
        out_shape=tuple(jax.ShapeDtypeStruct(x.shape, x.dtype) for x in results),
        in_specs=[anywhere] * 5,
        out_specs=(anywhere,) * 5,
        scratch_shapes=[dma((5,))],
        compiler_params=pltpu.CompilerParams(vmem_limit_bytes=1 << 20),
    )(*results)


def shift(block, distance):
    n = lax.axis_size("seq")
    route = [(i, i + distance) for i in range(n) if 0 <= i + distance < n]
    return lax.ppermute(block, "seq", route)


def swap(block, axis, bit):
    n = lax.axis_size(axis)
    return lax.ppermute(block, axis, [(i, i ^ bit) for i in range(n)])


def gather_heads(block, first):
    me = lax.axis_index("head")
    bit = lax.axis_size("head") // 2
    columns = block.shape[1]
    held = [block]
    while bit:
        other = swap(jnp.concatenate(held, axis=1), "head", bit)
        if first is not None:
            other, first = lax.optimization_barrier((other, first))
            first = None
        high = (me // bit) % 2 == 1
        merged = []
        for i, own in enumerate(held):
            theirs = other[:, i * columns : (i + 1) * columns]
            merged += [jnp.where(high, theirs, own), jnp.where(high, own, theirs)]
        held = merged
        bit //= 2
    return held


def scatter_heads(partial):
    me = lax.axis_index("head")
    size = lax.axis_size("head")
    share = partial.shape[1] // size
    held = [partial[:, i * share : (i + 1) * share] for i in range(size)]
    bit = 1
    while bit < size:
        high = (me // bit) % 2 == 1
        couples = list(zip(held[0::2], held[1::2]))
        given = jnp.concatenate([jnp.where(high, a, b).astype(BF) for a, b in couples], axis=1)
        other = swap(given, "head", bit)
        held = [
            jnp.where(high, b, a) + other[:, i * share : (i + 1) * share].astype(F32)
            for i, (a, b) in enumerate(couples)
        ]
        bit *= 2
    return held[0].astype(BF)


def with_doc(state, doc):
    rows = jnp.broadcast_to(doc.astype(BF)[:, None], (16, state.shape[-1]))
    return jnp.concatenate([state.astype(BF).reshape(-1, state.shape[-1]), rows], axis=0)


def window(total, sign, first=None):
    rows = lax.broadcasted_iota(jnp.int32, (total.shape[0], 1), 0) < total.shape[0] - 16
    span = 1
    while span < lax.axis_size("seq") // 2:
        far = shift(total, sign * span)
        if first is not None and 4 * span >= lax.axis_size("seq"):
            far, first = lax.optimization_barrier((far, first))
        same = (far[-16:-15] == total[-16:-15]) & rows
        total = total + jnp.where(same, far, jnp.zeros_like(far))
        span *= 2
    return total


def plain(queries, key_vectors, value_vectors, doc_ids, out_weight, grad_out):
    n = lax.axis_size("seq")
    m = lax.axis_size("head")
    length, heads, dh = queries.shape
    place = lax.axis_index("seq")
    parity = place % 2
    line = n // 2
    where_on_line = place // 2
    columns = out_weight.shape[1]
    width = columns // n

    docs = doc_ids.astype(F32)
    tail = (docs == docs[-1]).astype(BF)
    own_state = jnp.einsum(
        "shd,she->hde", key_vectors * tail[:, None, None], value_vectors, preferred_element_type=F32
    )
    near_flat = shift(with_doc(own_state, docs[-1:]), 1)
    own_gathered = gather_heads(grad_out, near_flat)
    near_flat, grad_out = lax.optimization_barrier((near_flat, grad_out))
    flat = window(near_flat, 1)
    before = flat[-16, :1].astype(F32)
    state_low = flat[:-16].reshape(own_state.shape)

    causal = lax.broadcasted_iota(jnp.int32, (length, length), 0) >= lax.broadcasted_iota(
        jnp.int32, (length, length), 1
    )
    pairs = causal & (docs[:, None] == docs[None, :])
    reads = (docs == before[0]).astype(F32)
    scores = jnp.einsum("thd,shd->hts", queries, key_vectors, preferred_element_type=F32)
    scores_low = jnp.where(pairs[None], scores, 0.0).astype(BF)
    attn = jnp.einsum("hts,she->the", scores_low, value_vectors, preferred_element_type=F32)
    attn = attn + reads[:, None, None] * jnp.einsum(
        "thd,hde->the", queries, state_low, preferred_element_type=F32
    )
    scale = lax.rsqrt(jnp.mean(attn * attn, axis=-1, keepdims=True) + 1e-05)
    normed_f = attn * scale
    normed = normed_f.astype(BF).reshape(length, -1)
    partner_normed = swap(normed, "seq", 1)

    share = columns // m
    odd = parity == 1
    for_partner = [
        jnp.where(odd, grad_out[:, i : i + width], grad_out[:, i + width : i + 2 * width])
        for i in range(0, share, 2 * width)
    ]
    from_partner = swap(jnp.concatenate(for_partner, axis=1), "seq", 1)
    cotangent = jnp.concatenate(own_gathered, axis=1)
    partner_cot = jnp.concatenate(gather_heads(from_partner, normed), axis=1)

    grad_normed = lax.dot_general(
        cotangent, out_weight, (((1,), (1,)), ((), ())), preferred_element_type=F32
    ).reshape(attn.shape)
    grad_attn = (
        scale * (grad_normed - normed_f * jnp.mean(grad_normed * normed_f, axis=-1, keepdims=True))
    ).astype(BF)
    head_mask = (docs == docs[0]).astype(BF)
    own_back = jnp.einsum(
        "thd,the->hde", queries * head_mask[:, None, None], grad_attn, preferred_element_type=F32
    )
    near_flat = shift(with_doc(own_back, docs[:1]), -1)

    def share_of(step):
        goal = (where_on_line + step) % line
        mine = lax.dynamic_slice_in_dim(cotangent, (2 * goal + parity) * width, width, 1)
        theirs = lax.dynamic_slice_in_dim(partner_cot, goal * width, width, 1)
        over_tokens = (((0,), (0,)), ((), ()))
        return lax.dot_general(
            normed, mine, over_tokens, preferred_element_type=F32
        ) + lax.dot_general(partner_normed, theirs, over_tokens, preferred_element_type=F32)

    terms = [share_of(step).astype(BF) for step in range(1, line)]
    terms, near_flat = lax.optimization_barrier((terms, near_flat))
    terms, grad_attn_in, normed_out = lax.optimization_barrier((terms, grad_attn, normed))
    partial_out = jnp.dot(normed_out, out_weight, preferred_element_type=F32)
    layer_out = scatter_heads(partial_out)
    flat = window(near_flat, -1, layer_out)
    after = flat[-16, :1].astype(F32)
    back_low = flat[:-16].reshape(own_back.shape)
    writes = (docs == after[0]).astype(F32)
    arrived = []
    for step, term in enumerate(terms, 1):
        route = [
            (2 * a + b, 2 * ((a + step) % line) + b) for a in range(line) for b in range(2)
        ]
        arrived.append(lax.ppermute(term, "seq", route))
    own_term = share_of(0)

    grad_scores = jnp.einsum("the,she->hts", grad_attn_in, value_vectors, preferred_element_type=F32)
    grad_scores = jnp.where(pairs[None], grad_scores, 0.0).astype(BF)
    grad_queries = jnp.einsum("hts,shd->thd", grad_scores, key_vectors, preferred_element_type=F32)
    grad_queries = grad_queries + reads[:, None, None] * jnp.einsum(
        "the,hde->thd", grad_attn_in, state_low, preferred_element_type=F32
    )
    grad_keys = jnp.einsum("hts,thd->shd", grad_scores, queries, preferred_element_type=F32)
    grad_keys = grad_keys + writes[:, None, None] * jnp.einsum(
        "she,hde->shd", value_vectors, back_low, preferred_element_type=F32
    )
    grad_values = jnp.einsum("hts,the->she", scores_low, grad_attn_in, preferred_element_type=F32)
    grad_values = grad_values + writes[:, None, None] * jnp.einsum(
        "shd,hde->she", key_vectors, back_low, preferred_element_type=F32
    )
    arrived, layer_out = lax.optimization_barrier((arrived, layer_out))
    grad_weight = own_term
    for part in arrived:
        grad_weight = grad_weight + part.astype(F32)
    return (
        layer_out,
        grad_queries.astype(BF),
        grad_keys.astype(BF),
        grad_values.astype(BF),
        grad_weight,
    )


def fits(mesh, columns, heads, dh):
    n, m = mesh.shape["seq"], mesh.shape["head"]
    lanes = 128
    return m == 4 and n == 2 * m and columns % (lanes * n) == 0 and heads % 2 == 0 and dh == lanes


def choose(mesh):
    def shards(queries, key_vectors, value_vectors, doc_ids, out_weight, grad_out):
        heads, dh = queries.shape[1:]
        form = fused if fits(mesh, out_weight.shape[1], heads, dh) else plain
        return form(queries, key_vectors, value_vectors, doc_ids, out_weight, grad_out)

    return shards


def solution(mesh):
    placed = (
        P("seq", "head", None),
        P("seq", "head", None),
        P("seq", "head", None),
        P("seq"),
        P("head", None),
        P("seq", "head"),
    )
    return jax.shard_map(
        choose(mesh),
        mesh=mesh,
        in_specs=placed,
        out_specs=(
            P("seq", "head"),
            P("seq", "head", None),
            P("seq", "head", None),
            P("seq", "head", None),
            P("head", "seq"),
        ),
        check_vma=False,
    )
```
